512 devices in a mesh: grp: 8 (over y), dev: 64 (over z, x, core).
Axes of the slice: x: 4, y: 8, z: 8, core: 2. Of those that a mesh axis runs over, the one named last changes fastest.
Arguments:
- leaf_right: float32 [32, 131072], P(None, ('grp', 'dev')), may hold values from -6 to 6
- leaf_inverse: float32 [1024, 128, 128], P(('grp', 'dev')), may hold values from -1 to 2, as said below
- leaf_link: float32 [1024, 128, 128], P(('grp', 'dev')), may hold values from -0.25 to 0.25
- leaf_front: float32 [1024, 128, 128], P(('grp', 'dev')), may hold values from -0.1875 to 0.1875
- parents: int32 [1024], P(('grp', 'dev')), may hold values from 1 to 2, as said below
- front_rows: int32 [1024], P(('grp', 'dev')), may hold values from 0 to 15
- live_blocks: int32 [512], P(('grp', 'dev')), may hold values from 1 to 2, 896 in all
- front_right: float32 [32, 16384], P(None, ('grp', 'dev')), may hold values from -6 to 6
- front_inverse: float32 [16384, 2048], P(('grp', 'dev')), may hold values from -1 to 2, as said below
- front_couple: float32 [16384, 4096], P(('grp', 'dev')), may hold values from -0.046875 to 0.046875
- root_right: float32 [32, 2, 2048], P(None, None, 'dev'), may hold values from -6 to 6
- root_inverse: float32 [2, 2048, 2048], P(None, 'dev', 'grp'), may hold values from -1 to 2, as said below
- root_couple: float32 [1, 2048, 2048], P(None, 'dev', 'grp'), may hold values from -0.09375 to 0.09375
Outputs:
- leaf_solution: float32 [32, 131072], P(None, ('grp', 'dev'))
- front_solution: float32 [32, 16384], P(None, 'grp')
- root_solution: float32 [32, 2, 2048], P(None, None, 'dev')
The draws below stay inside these ranges and needn't reach their ends.
Inputs may be any that keep to these rules, and one draw needn't show every extreme that they name: For local block k = b mod 2, parents[b] lies in k + 1 .. 2; the value 2 means no parent among the piece's blocks. A piece's live blocks are its first live_blocks[p]; some piece has all 2. `leaf_inverse`: each block is lower triangular with a positive diagonal. `front_inverse`: each front's block is lower triangular with a positive diagonal. `root_inverse`: each level's block is lower triangular with a positive diagonal.
All inputs are finite; a program needn't handle non-finite values.
Results may differ from the reference program's by a relative error of at most 0.0003.
Values sent between devices are 32-bit elements; how exact they have to be, the bound alone decides.
No kernel may reach another device: no remote copies, remote signals or barrier semaphores. Data moves between devices by JAX's collectives and lax.ppermute only.
A program may use at most 64 MiB of HBM per device.

```python
import math
import jax
import jax.numpy as jnp
import numpy as np
from jax import lax

NB = 128
RIGHT_SIDES = 32
SB = 2
FBG = 16
CHAIN_LEVELS = 2
FG = 2048
LEVEL_ROWS = 2048
DEVS = 512
NSUB = 1024
GROWS = 16384
NPAIR = 1
FEEDS = 8
LIVE_TOTAL = 896
N_GRP = 8
N_DEV = 64


def lower_inverse(key, salt, blocks_count, order):
    first_key, second_key = jax.random.split(jax.random.fold_in(key, salt))
    scales = jnp.exp(jax.random.uniform(first_key, (blocks_count, order), jnp.float32, math.log(0.6), math.log(1.4)))
    noise = jax.random.normal(second_key, (blocks_count, order, order), jnp.float32)
    noise = jnp.clip(noise, -4.0, 4.0)
    lower = jnp.tril(noise * (0.5 / math.sqrt(order)), -1)
    return lower + jnp.eye(order, dtype=jnp.float32)[None] * scales[:, None, :]


def draw_leaf_inverse(key, part):
    return lower_inverse(key, 17, NSUB, NB)


def draw_front_inverse(key, part):
    return lower_inverse(key, 23, GROWS // FG, FG).reshape(GROWS, FG)


def draw_root_inverse(key, part):
    return lower_inverse(key, 31, CHAIN_LEVELS, LEVEL_ROWS)


def draw_parents(key, part):
    place = jnp.arange(NSUB, dtype=jnp.int32) % SB
    spans = SB - place
    offsets = jax.random.randint(jax.random.fold_in(key, 29), (NSUB,), 0, spans, dtype=jnp.int32)
    return (place + 1 + offsets).astype(jnp.int32)


def set_ends(values, rng, least, largest):
    spot = [jax.random.randint(jax.random.fold_in(rng, axis), (), 0, length) for axis, length in enumerate(values.shape)]
    longest = values.shape.index(max(values.shape))
    beside = spot[:longest] + [(spot[longest] + 1) % values.shape[longest]] + spot[longest + 1:]
    return values.at[tuple(spot)].set(least).at[tuple(beside)].set(largest)


def levels(key, dims, shards, smallest, top_value):
    def one(dim, parts):
        heights = jax.random.uniform(jax.random.fold_in(jax.random.fold_in(key, 6), dim), (parts,), jnp.float32, smallest / len(shards), top_value / len(shards))
        return jnp.repeat(jnp.exp(heights), dims[dim] // parts).reshape((-1,) + (1,) * (len(dims) - dim - 1))

    level = one(*shards[0])
    for cut in shards[1:]:
        level = level * one(*cut)
    return level


def length_profile(number_of, total, most, slope):
    portions = [(1 << 20) // math.isqrt(grade ** slope) + 1 for grade in range(2, number_of + 1)]
    spare, counts = total - most - (number_of - 1), [1] * (number_of - 1)
    while spare > 0:
        free = [i for i in range(number_of - 1) if counts[i] < most]
        mass, left = sum([portions[i] for i in free]), spare
        for i in free:
            more = min(most - counts[i], max(1, left * portions[i] // mass), spare)
            counts[i] = counts[i] + more
            spare = spare - more
    return np.array([most] + counts)


def uneven(own_key, count, total, most, skew):
    if count == 2:
        one = jax.random.randint(own_key, (), max(1, total - most), min(most, total - 1) + 1)
        return jnp.stack([one, total - one])
    tallies = jnp.asarray(length_profile(count, total, most, skew), jnp.int32)
    couples = (count - 1) // 2
    donor, taker = tallies[1:1 + 2 * couples:2], tallies[2:2 + 2 * couples:2]
    room = jnp.minimum(donor - 1, most - taker)
    moved = jax.random.randint(jax.random.fold_in(own_key, 1), (couples,), 0, 1 << 20) % (room + 1)
    tallies = tallies.at[1:1 + 2 * couples:2].set(donor - moved).at[2:2 + 2 * couples:2].set(taker + moved)
    return tallies[jax.random.permutation(jax.random.fold_in(own_key, 2), count)]


def gaussian(rng, shape, width, bound, shards=(), held_as=jnp.bfloat16):
    entries = width * jax.random.normal(rng, shape, jnp.float32)
    if shards:
        entries = entries * levels(rng, shape, shards, -0.22, 0.18)
    return jnp.clip(entries, -bound, bound).astype(held_as)


def setup_inputs(seed: int = 0) -> dict:
    streams_of = jax.random.split(jax.random.key(seed), 14)
    return {
        "leaf_right": gaussian(streams_of[0], (RIGHT_SIDES, NSUB * NB), 1.0, 6.0, ((1, 512),), jnp.float32),
        "leaf_inverse": draw_leaf_inverse(jax.random.fold_in(streams_of[13], 71), 0),
        "leaf_link": gaussian(streams_of[2], (NSUB, NB, NB), (4 * NB) ** -0.5, 0.25, ((0, 512),), jnp.float32),
        "leaf_front": gaussian(streams_of[3], (NSUB, NB, NB), (NB * FEEDS) ** -0.5, 0.1875, ((0, 512),), jnp.float32),
        "parents": draw_parents(jax.random.fold_in(streams_of[13], 71), 0),
        "front_rows": set_ends(jax.random.randint(streams_of[5], (NSUB,), 0, FBG), jax.random.fold_in(streams_of[5], 1), 0, FBG - 1).astype(jnp.int32),
        "live_blocks": uneven(streams_of[6], DEVS, LIVE_TOTAL, SB, 2).astype(jnp.int32),
        "front_right": gaussian(streams_of[7], (RIGHT_SIDES, GROWS), 1.0, 6.0, ((1, 512),), jnp.float32),
        "front_inverse": draw_front_inverse(jax.random.fold_in(streams_of[13], 71), 0),
        "front_couple": gaussian(streams_of[9], (GROWS, CHAIN_LEVELS * LEVEL_ROWS), GROWS ** -0.5, 0.046875, ((0, 512),), jnp.float32),
        "root_right": gaussian(streams_of[10], (RIGHT_SIDES, CHAIN_LEVELS, LEVEL_ROWS), 1.0, 6.0, ((2, 64),), jnp.float32),
        "root_inverse": draw_root_inverse(jax.random.fold_in(streams_of[13], 71), 0),
        "root_couple": gaussian(streams_of[12], (NPAIR, LEVEL_ROWS, LEVEL_ROWS), (LEVEL_ROWS * CHAIN_LEVELS) ** -0.5, 0.09375, ((1, 64), (2, 8)), jnp.float32),
    }


EXACT_ARITHMETIC = lax.Precision.HIGHEST


def front_table(targets, blocks_front):
    return (targets[:, None] == jnp.arange(blocks_front, dtype=jnp.int32)[None, :]).astype(jnp.float32)


def piece_forward(right_side, inverse, linked, parents, live_count, upper_bound):
    total_blocks = inverse.shape[0]

    def advance(member, loop_state):
        pending, solved = loop_state
        is_alive = member < live_count
        residual = lax.dynamic_index_in_dim(right_side, member, 1, False) - lax.dynamic_index_in_dim(pending, member, 1, False)
        solved_block = jnp.where(is_alive, jnp.dot(residual, inverse[member], precision=EXACT_ARITHMETIC), 0.0)
        solved = lax.dynamic_update_index_in_dim(solved, solved_block, member, 1)
        target = parents[member]
        target_slot = jnp.minimum(target, total_blocks - 1)
        update = jnp.where(target < live_count, jnp.dot(solved_block, linked[member], precision=EXACT_ARITHMETIC), 0.0)
        current = lax.dynamic_index_in_dim(pending, target_slot, 1, False)
        pending = lax.dynamic_update_index_in_dim(pending, current + update, target_slot, 1)
        return pending, solved

    empty_state = jnp.zeros_like(right_side)
    return lax.fori_loop(0, upper_bound, advance, (empty_state, empty_state))[1]


def piece_backward(base_terms, inverse, linked, parents, live_count, upper_bound):
    total_blocks = inverse.shape[0]

    def retreat(turn_index, solved):
        member = upper_bound - 1 - turn_index
        is_alive = member < live_count
        target = parents[member]
        target_slot = jnp.minimum(target, total_blocks - 1)
        parent_value = lax.dynamic_index_in_dim(solved, target_slot, 1, False)
        carried = jnp.where(target < live_count, jnp.einsum("rn,mn->rm", parent_value, linked[member], precision=EXACT_ARITHMETIC), 0.0)
        residual = lax.dynamic_index_in_dim(base_terms, member, 1, False) - carried
        solved_block = jnp.where(is_alive, jnp.einsum("rn,mn->rm", residual, inverse[member], precision=EXACT_ARITHMETIC), 0.0)
        return lax.dynamic_update_index_in_dim(solved, solved_block, member, 1)

    return lax.fori_loop(0, upper_bound, retreat, jnp.zeros_like(base_terms))


def front_update(solved, coupled, targets, blocks_front):
    contrib = jnp.einsum("rkn,knm->rkm", solved, coupled, precision=EXACT_ARITHMETIC)
    table = front_table(targets, blocks_front)
    placed = jnp.einsum("rkm,kf->rfm", contrib, table, precision=EXACT_ARITHMETIC)
    return placed.reshape(solved.shape[0], -1)


def front_back(front_values, coupled, targets, blocks_front):
    table = front_table(targets, blocks_front)
    grouped = front_values.reshape(front_values.shape[0], blocks_front, -1)
    picked = jnp.einsum("rfn,kf->rkn", grouped, table, precision=EXACT_ARITHMETIC)
    return jnp.einsum("rkn,kmn->rkm", picked, coupled, precision=EXACT_ARITHMETIC)


def reference(leaf_right, leaf_inverse, leaf_link, leaf_front, parents, front_rows, live_blocks, front_right, front_inverse, front_couple, root_right, root_inverse, root_couple):
    right_pieces = leaf_right.reshape(RIGHT_SIDES, DEVS, SB, NB)
    inverse_pieces = leaf_inverse.reshape(DEVS, SB, NB, NB)
    link_pieces = leaf_link.reshape(DEVS, SB, NB, NB)
    front_pieces = leaf_front.reshape(DEVS, SB, NB, NB)
    parent_pieces = parents.reshape(DEVS, SB)
    target_pieces = front_rows.reshape(DEVS, SB)

    def forward_one(right_side, inverse, linked, coupled, parent_row, target_row, live_count):
        solved = piece_forward(right_side, inverse, linked, parent_row, live_count, SB)
        return solved, front_update(solved, coupled, target_row, FBG)

    solved_all, updates = jax.vmap(forward_one, in_axes=(1, 0, 0, 0, 0, 0, 0))(right_pieces, inverse_pieces, link_pieces, front_pieces, parent_pieces, target_pieces, live_blocks)
    group_updates = jnp.sum(updates.reshape(N_GRP, N_DEV, RIGHT_SIDES, FG), axis=1)
    group_right = jnp.transpose(front_right.reshape(RIGHT_SIDES, N_GRP, FG), (1, 0, 2))
    group_inverse = front_inverse.reshape(N_GRP, FG, FG)
    group_coupling_block = front_couple.reshape(N_GRP, FG, CHAIN_LEVELS * LEVEL_ROWS)
    forward_front_sweep = jnp.einsum("grf,gfh->grh", group_right - group_updates, group_inverse, precision=EXACT_ARITHMETIC)
    raised_values = jnp.einsum("dpl,dlt->pt", forward_front_sweep, group_coupling_block, precision=EXACT_ARITHMETIC).reshape(RIGHT_SIDES, CHAIN_LEVELS, LEVEL_ROWS)

    forward_values = [None] * CHAIN_LEVELS
    for height in reversed(range(CHAIN_LEVELS)):
        residual = root_right[:, height] - raised_values[:, height]
        for upper_level in range(height + 1, CHAIN_LEVELS):
            residual = residual - jnp.einsum("rj,ij->ri", forward_values[upper_level], root_couple[upper_level * (upper_level - 1) // 2 + height], precision=EXACT_ARITHMETIC)
        forward_values[height] = jnp.dot(residual, root_inverse[height], precision=EXACT_ARITHMETIC)
    back_values = [None] * CHAIN_LEVELS
    for height in range(CHAIN_LEVELS):
        residual = forward_values[height]
        for lower_level in range(height):
            residual = residual - jnp.dot(back_values[lower_level], root_couple[height * (height - 1) // 2 + lower_level], precision=EXACT_ARITHMETIC)
        back_values[height] = jnp.einsum("rj,ij->ri", residual, root_inverse[height], precision=EXACT_ARITHMETIC)
    root_solution = jnp.stack(back_values, 1)

    flattened_root = root_solution.reshape(RIGHT_SIDES, CHAIN_LEVELS * LEVEL_ROWS)
    backward_remainder = forward_front_sweep - jnp.einsum("sv,dmv->dsm", flattened_root, group_coupling_block, precision=EXACT_ARITHMETIC)
    front_values = jnp.einsum("grh,gfh->grf", backward_remainder, group_inverse, precision=EXACT_ARITHMETIC)
    front_solution = jnp.transpose(front_values, (1, 0, 2)).reshape(RIGHT_SIDES, N_GRP * FG)
    piece_fronts = jnp.repeat(front_values, N_DEV, axis=0)

    def backward_one(solved, inverse, linked, coupled, parent_row, target_row, live_count, front_piece):
        base_terms = solved - front_back(front_piece, coupled, target_row, FBG)
        return piece_backward(base_terms, inverse, linked, parent_row, live_count, SB)

    leaf_all = jax.vmap(backward_one)(solved_all, inverse_pieces, link_pieces, front_pieces, parent_pieces, target_pieces, live_blocks, piece_fronts)
    leaf_solution = jnp.transpose(leaf_all, (1, 0, 2, 3)).reshape(RIGHT_SIDES, NSUB * NB)
    return leaf_solution, front_solution, root_solution
```

```python
import jax
import jax.numpy as jnp
from jax import lax
from jax.sharding import Mesh
from jax.sharding import PartitionSpec as P

EXACT = lax.Precision.HIGHEST
NEAR = ("x", "core")
DEV = ("z", "x", "core")


def mm(left, right):
    return jnp.dot(left, right, precision=EXACT)


def mmt(left, right):
    return jnp.einsum("rn,mn->rm", left, right, precision=EXACT)


def swap(chunks, axes):
    return lax.all_to_all(chunks, axes, 0, 0, tiled=True)


def spread(values, axes, count):
    return swap(jnp.broadcast_to(values[None], (count,) + values.shape), axes)


def reduce_over(values, axes, count):
    return jnp.sum(spread(values, axes, count), 0)


def scatter_sum(values, axes, count):
    rows, width = values.shape
    chunks = values.reshape(rows, count, width // count).transpose(1, 0, 2)
    return jnp.sum(swap(chunks, axes), 0)


def gather_columns(values, axes, count):
    rows, width = values.shape
    return spread(values, axes, count).transpose(1, 0, 2).reshape(rows, count * width)


def make_body(sizes):
    n_grp, n_z = sizes["grp"], sizes["z"]
    n_near = sizes["x"] * sizes["core"]
    n_dev = n_z * n_near

    def reduce_dev(values):
        return reduce_over(reduce_over(values, NEAR, n_near), "z", n_z)

    def body(
        leaf_right,
        leaf_inverse,
        leaf_link,
        leaf_front,
        parents,
        front_rows,
        live_blocks,
        front_right,
        front_inverse,
        front_couple,
        root_right,
        root_inverse,
        root_couple,
    ):
        rows = leaf_right.shape[0]
        width = leaf_inverse.shape[1]
        front_order = front_inverse.shape[1]
        n_front = front_order // width
        share = root_right.shape[2]
        live = live_blocks[0]
        has_parent = parents[0] < live
        right0, right1 = leaf_right[:, :width], leaf_right[:, width:]
        solved0 = jnp.where(live > 0, mm(right0, leaf_inverse[0]), 0.0)
        lifted = jnp.where(has_parent, mm(solved0, leaf_link[0]), 0.0)
        solved1 = jnp.where(live > 1, mm(right1 - lifted, leaf_inverse[1]), 0.0)
        given0, given1 = mm(solved0, leaf_front[0]), mm(solved1, leaf_front[1])
        slots = jnp.arange(n_front, dtype=jnp.int32)[None, :, None]
        placed = jnp.where(slots == front_rows[0], given0[:, None, :], 0.0) + jnp.where(
            slots == front_rows[1], given1[:, None, :], 0.0
        )
        update = scatter_sum(placed.reshape(rows, front_order), DEV, n_dev)
        terms = mm(front_right - update, front_inverse)
        y_front = scatter_sum(terms, DEV, n_dev)

        raised = mm(y_front, front_couple).reshape(rows, 2, n_dev, share)
        raised = jnp.sum(swap(raised.transpose(2, 0, 1, 3).reshape(n_dev, rows, 2 * share), DEV), 0)
        raised = reduce_over(raised, "grp", n_grp)
        low = root_right[:, 0] - raised[:, :share]
        high = root_right[:, 1] - raised[:, share:]
        w_low, w_high, link = root_inverse[0], root_inverse[1], root_couple[0]
        y_high = reduce_dev(mm(high, w_high))
        low = low - reduce_over(mmt(y_high, link), "grp", n_grp)
        y_low = reduce_dev(mm(low, w_low))
        x_low = reduce_over(mmt(y_low, w_low), "grp", n_grp)
        y_high = y_high - reduce_dev(mm(x_low, link))
        x_high = reduce_over(mmt(y_high, w_high), "grp", n_grp)

        both = jnp.concatenate([x_low, x_high], 1)
        whole = spread(both, DEV, n_dev).reshape(n_dev, rows, 2, share)
        whole = whole.transpose(1, 2, 0, 3).reshape(rows, 2 * n_dev * share)
        rest = y_front - mmt(whole, front_couple)
        rest = gather_columns(rest, DEV, n_dev)
        front_solution = gather_columns(mmt(rest, front_inverse), DEV, n_dev)

        def back(solved, block):
            start = front_rows[block] * width
            picked = lax.dynamic_slice(front_solution, (0, start), (rows, width))
            return solved - mmt(picked, leaf_front[block])

        base0, base1 = back(solved0, 0), back(solved1, 1)
        leaf1 = jnp.where(live > 1, mmt(base1, leaf_inverse[1]), 0.0)
        carried = jnp.where(has_parent, mmt(leaf1, leaf_link[0]), 0.0)
        leaf0 = jnp.where(live > 0, mmt(base0 - carried, leaf_inverse[0]), 0.0)
        leaf_solution = jnp.concatenate([leaf0, leaf1], 1)
        return leaf_solution, front_solution, jnp.stack([x_low, x_high], 1)

    return body


def solution(mesh):
    n_grp, n_dev = mesh.shape["grp"], mesh.shape["dev"]
    fine = Mesh(mesh.devices.reshape(n_grp, n_dev // 8, 4, 2), ("grp", "z", "x", "core"))
    every = ("grp",) + DEV
    in_specs = (
        P(None, every),
        P(every, None, None),
        P(every, None, None),
        P(every, None, None),
        P(every),
        P(every),
        P(every),
        P(None, every),
        P(every, None),
        P(every, None),
        P(None, None, DEV),
        P(None, DEV, "grp"),
        P(None, DEV, "grp"),
    )
    out_specs = (P(None, every), P(None, "grp"), P(None, None, DEV))
    body = make_body(dict(fine.shape))
    return jax.shard_map(body, mesh=fine, in_specs=in_specs, out_specs=out_specs, check_vma=False)
```

```python
import jax
import jax.numpy as jnp
from jax import lax
from jax.sharding import Mesh
from jax.sharding import PartitionSpec as P

EXACT = lax.Precision.HIGH
NEAR = ("x", "core")
DEV = ("z", "x", "core")


def mm(left, right):
    return jnp.dot(left, right, precision=EXACT)


def mmt(left, right):
    return jnp.einsum("rn,mn->rm", left, right, precision=EXACT)


def swap(chunks, axes):
    return lax.all_to_all(chunks, axes, 0, 0, tiled=True)


def spread(values, axes, count):
    return swap(jnp.broadcast_to(values[None], (count,) + values.shape), axes)


def reduce_over(values, axes, count):
    return jnp.sum(spread(values, axes, count), 0)


def make_body(sizes):
    n_grp, n_z = sizes["grp"], sizes["z"]
    n_near = sizes["x"] * sizes["core"]
    n_dev = n_z * n_near

    def body(
        leaf_right,
        leaf_inverse,
        leaf_link,
        leaf_front,
        parents,
        front_rows,
        live_blocks,
        front_right,
        front_inverse,
        front_couple,
        root_right,
        root_inverse,
        root_couple,
    ):
        rows = leaf_right.shape[0]
        width = leaf_inverse.shape[1]
        front_order = front_inverse.shape[1]
        n_front = front_order // width
        share = front_inverse.shape[0]
        slab = share * n_z
        part = root_inverse.shape[2]
        live = live_blocks[0]
        my_z = lax.axis_index("z")

        def near_sum(natural):
            chunks = natural.reshape(rows, n_z, n_near, share).transpose(2, 0, 1, 3)
            return jnp.sum(swap(chunks.reshape(n_near, rows, slab), NEAR), 0)

        def own(values):
            return lax.dynamic_slice_in_dim(values, my_z * share, share, 1)

        blocks = front_inverse.reshape(share, n_z, part).transpose(1, 0, 2)
        wide = jnp.concatenate([blocks, root_inverse, root_couple], 0)
        wide = lax.all_gather(wide, "z", axis=1, tiled=True)
        front_slab, w_low, w_high, link = wide[:n_z], wide[n_z], wide[n_z + 1], wide[n_z + 2]

        has_parent = parents[0] < live
        right0, right1 = leaf_right[:, :width], leaf_right[:, width:]
        solved0 = jnp.where(live > 0, mm(right0, leaf_inverse[0]), 0.0)
        lifted = jnp.where(has_parent, mm(solved0, leaf_link[0]), 0.0)
        solved1 = jnp.where(live > 1, mm(right1 - lifted, leaf_inverse[1]), 0.0)
        given0, given1 = mm(solved0, leaf_front[0]), mm(solved1, leaf_front[1])
        slots = jnp.arange(n_front, dtype=jnp.int32)[None, :, None]
        placed = jnp.where(slots == front_rows[0], given0[:, None, :], 0.0) + jnp.where(
            slots == front_rows[1], given1[:, None, :], 0.0
        )
        update = near_sum(placed.reshape(rows, front_order))
        here = (jnp.arange(slab, dtype=jnp.int32) // share == my_z)[None, :]
        start = jnp.where(here, jnp.tile(front_right, (1, n_z)), 0.0) - update
        start = jnp.broadcast_to(reduce_over(start, "z", n_z)[None], (n_z, rows, slab))
        terms = jnp.einsum("zrk,zkn->zrn", start, front_slab, precision=EXACT)
        terms = lax.optimization_barrier(terms).reshape(n_z, rows, n_near, share)
        terms = terms.transpose(2, 1, 0, 3).reshape(n_near, rows, slab)
        y_slab = jnp.sum(swap(terms, NEAR), 0)
        y_own = own(y_slab)

        raised = mm(y_own, front_couple)
        half = rows // 2
        chunks = raised.reshape(2, half, 2, n_dev, share).transpose(3, 1, 0, 2, 4)
        raised = jnp.sum(swap(chunks.reshape(n_dev, half, 4 * share), DEV), 0)
        given = root_right.reshape(2, half, 2, share).transpose(1, 0, 2, 3).reshape(half, 4 * share)
        given = jnp.where(lax.axis_index("grp") == 0, given, 0.0) - raised
        given = jnp.sum(spread(given, ("grp", "z"), n_grp * n_z).reshape(n_grp, n_z, half, 4 * share), 0)
        given = given.reshape(n_z, half, 2, 2, share).transpose(3, 2, 1, 0, 4).reshape(2, rows, slab)
        low, high = given[0], given[1]
        y_high = reduce_over(mm(high, w_high), NEAR, n_near)
        low = low - reduce_over(mmt(y_high, link), "grp", n_grp)
        y_low = reduce_over(mm(low, w_low), NEAR, n_near)
        x_low = reduce_over(mmt(y_low, w_low), "grp", n_grp)
        y_high = y_high - reduce_over(mm(x_low, link), NEAR, n_near)
        x_high = reduce_over(mmt(y_high, w_high), "grp", n_grp)

        both = jnp.concatenate([x_low, x_high], 1)
        whole = spread(both, NEAR, n_near).reshape(n_near, rows, 2, n_z, share)
        whole = whole.transpose(1, 2, 3, 0, 4).reshape(rows, 2 * front_order)
        rest = y_own - mmt(whole, front_couple)
        rest = rest.reshape(4, rows // 4, share).transpose(1, 0, 2).reshape(rows // 4, 4 * share)
        rest = spread(rest, DEV, n_dev).reshape(n_dev, rows // 4, 4, share)
        rest = rest.reshape(n_z, n_near, rows // 4, 4, share)
        rest = rest.transpose(0, 3, 2, 1, 4).reshape(n_z, rows, part)
        solved = jnp.einsum("zrn,zkn->zrk", rest, front_slab, precision=EXACT)
        front_solution = spread(jnp.sum(solved, 0), NEAR, n_near)
        front_solution = front_solution.reshape(n_near, rows, n_z, share)
        front_solution = front_solution.transpose(1, 2, 0, 3).reshape(rows, front_order)

        def back(solved, block):
            picked = lax.dynamic_slice(front_solution, (0, front_rows[block] * width), (rows, width))
            return solved - mmt(picked, leaf_front[block])

        base0, base1 = back(solved0, 0), back(solved1, 1)
        leaf1 = jnp.where(live > 1, mmt(base1, leaf_inverse[1]), 0.0)
        carried = jnp.where(has_parent, mmt(leaf1, leaf_link[0]), 0.0)
        leaf0 = jnp.where(live > 0, mmt(base0 - carried, leaf_inverse[0]), 0.0)
        leaf_solution = jnp.concatenate([leaf0, leaf1], 1)
        return leaf_solution, front_solution, jnp.stack([own(x_low), own(x_high)], 1)

    return body


def solution(mesh):
    n_grp, n_dev = mesh.shape["grp"], mesh.shape["dev"]
    fine = Mesh(mesh.devices.reshape(n_grp, n_dev // 8, 4, 2), ("grp", "z", "x", "core"))
    every = ("grp",) + DEV
    in_specs = (
        P(None, every),
        P(every, None, None),
        P(every, None, None),
        P(every, None, None),
        P(every),
        P(every),
        P(every),
        P(None, every),
        P(every, None),
        P(every, None),
        P(None, None, DEV),
        P(None, DEV, "grp"),
        P(None, DEV, "grp"),
    )
    out_specs = (P(None, every), P(None, "grp"), P(None, None, DEV))
    body = make_body(dict(fine.shape))
    return jax.shard_map(body, mesh=fine, in_specs=in_specs, out_specs=out_specs, check_vma=False)
```

```python
import jax
import jax.numpy as jnp
from jax import lax
from jax.sharding import Mesh
from jax.sharding import PartitionSpec as P

EXACT = lax.Precision.HIGHEST
NEAR = ("x", "core")
DEV = ("z", "x", "core")


def mm(left, right):
    return jnp.dot(left, right, precision=EXACT)


def mmt(left, right):
    return jnp.einsum("rn,mn->rm", left, right, precision=EXACT)


def swap(chunks, axes):
    return lax.all_to_all(chunks, axes, 0, 0, tiled=True)


def spread(values, axes, count):
    return swap(jnp.broadcast_to(values[None], (count,) + values.shape), axes)


def reduce_over(values, axes, count):
    return jnp.sum(spread(values, axes, count), 0)


def fold(values, folds):
    rows, width = values.shape
    tall = rows // folds
    return values.reshape(folds, tall, width).transpose(1, 0, 2).reshape(tall, folds * width)


def unfold(values, folds):
    tall, width = values.shape
    thin = width // folds
    return values.reshape(tall, folds, thin).transpose(1, 0, 2).reshape(folds * tall, thin)


def make_body(sizes):
    n_grp, n_z = sizes["grp"], sizes["z"]
    n_near = sizes["x"] * sizes["core"]
    n_dev = n_z * n_near

    def body(
        leaf_right,
        leaf_inverse,
        leaf_link,
        leaf_front,
        parents,
        front_rows,
        live_blocks,
        front_right,
        front_inverse,
        front_couple,
        root_right,
        root_inverse,
        root_couple,
    ):
        rows = leaf_right.shape[0]
        width = leaf_inverse.shape[1]
        front_order = front_inverse.shape[1]
        n_front = front_order // width
        share = front_inverse.shape[0]
        part = root_inverse.shape[2]
        few = rows // n_near
        live = live_blocks[0]
        my_dev = lax.axis_index(DEV)

        chain = jnp.concatenate([root_inverse, root_couple], 0)
        chain = spread(chain, NEAR, n_near).transpose(1, 0, 2, 3).reshape(3, n_near * share, part)

        def dev_sum(natural):
            chunks = natural.reshape(4, rows // 4, n_dev, share).transpose(2, 1, 0, 3)
            return unfold(jnp.sum(swap(chunks.reshape(n_dev, rows // 4, 4 * share), DEV), 0), 4)

        def dev_columns(values):
            chunks = spread(fold(values, 4), DEV, n_dev).reshape(n_dev, rows // 4, 4, share)
            return chunks.transpose(2, 1, 0, 3).reshape(rows, n_dev * share)

        has_parent = parents[0] < live
        right0, right1 = leaf_right[:, :width], leaf_right[:, width:]
        solved0 = jnp.where(live > 0, mm(right0, leaf_inverse[0]), 0.0)
        lifted = jnp.where(has_parent, mm(solved0, leaf_link[0]), 0.0)
        solved1 = jnp.where(live > 1, mm(right1 - lifted, leaf_inverse[1]), 0.0)
        given0, given1 = mm(solved0, leaf_front[0]), mm(solved1, leaf_front[1])
        slots = jnp.arange(n_front, dtype=jnp.int32)[None, :, None]
        placed = jnp.where(slots == front_rows[0], given0[:, None, :], 0.0) + jnp.where(
            slots == front_rows[1], given1[:, None, :], 0.0
        )
        placed, chain = lax.optimization_barrier((placed, chain))
        w_low, w_high, link = chain[0], chain[1], chain[2]
        start = front_right - dev_sum(placed.reshape(rows, front_order))
        y_own = dev_sum(mm(start, front_inverse))

        spots = my_dev * share + jnp.arange(share, dtype=jnp.int32)
        spots = jnp.concatenate([spots, front_order + spots])[:, None]
        picks = spots == jnp.arange(2 * front_order, dtype=jnp.int32)[None, :]
        picks = jnp.where(picks & (lax.axis_index("grp") == 0), 1.0, 0.0).astype(jnp.float32)
        fed = jnp.concatenate([-y_own, root_right[:, 0], root_right[:, 1]], 1)
        given = mm(fed, jnp.concatenate([front_couple, picks], 0))
        chunks = given.reshape(n_near, few, 2, n_z, part).transpose(3, 0, 2, 1, 4)
        given = jnp.sum(swap(chunks.reshape(n_dev, 2 * few, part), DEV), 0)
        given = reduce_over(given, "grp", n_grp)

        low, high = given[:few], given[few:]
        y_high = reduce_over(mm(high, w_high), "z", n_z)
        low = low - reduce_over(mmt(y_high, link), "grp", n_grp)
        y_low = reduce_over(mm(low, w_low), "z", n_z)
        x_low = reduce_over(mmt(y_low, w_low), "grp", n_grp)
        y_high = y_high - reduce_over(mm(x_low, link), "z", n_z)
        x_high = reduce_over(mmt(y_high, w_high), "grp", n_grp)

        whole = spread(jnp.concatenate([x_low, x_high], 0), DEV, n_dev)
        whole = whole.reshape(n_z, n_near, 2, few, part).transpose(1, 3, 2, 0, 4)
        whole = whole.reshape(rows, 2 * front_order)
        rest = dev_columns(y_own - mmt(whole, front_couple))
        front_solution = dev_columns(mmt(rest, front_inverse))

        def back(solved, block):
            picked = lax.dynamic_slice(front_solution, (0, front_rows[block] * width), (rows, width))
            return solved - mmt(picked, leaf_front[block])

        base0, base1 = back(solved0, 0), back(solved1, 1)
        leaf1 = jnp.where(live > 1, mmt(base1, leaf_inverse[1]), 0.0)
        carried = jnp.where(has_parent, mmt(leaf1, leaf_link[0]), 0.0)
        leaf0 = jnp.where(live > 0, mmt(base0 - carried, leaf_inverse[0]), 0.0)
        leaf_solution = jnp.concatenate([leaf0, leaf1], 1)
        root = whole.reshape(rows, 2, front_order)
        root = lax.dynamic_slice(root, (0, 0, my_dev * share), (rows, 2, share))
        return leaf_solution, front_solution, root

    return body


def solution(mesh):
    n_grp, n_dev = mesh.shape["grp"], mesh.shape["dev"]
    fine = Mesh(mesh.devices.reshape(n_grp, n_dev // 8, 4, 2), ("grp", "z", "x", "core"))
    every = ("grp",) + DEV
    in_specs = (
        P(None, every),
        P(every, None, None),
        P(every, None, None),
        P(every, None, None),
        P(every),
        P(every),
        P(every),
        P(None, every),
        P(every, None),
        P(every, None),
        P(None, None, DEV),
        P(None, DEV, "grp"),
        P(None, DEV, "grp"),
    )
    out_specs = (P(None, every), P(None, "grp"), P(None, None, DEV))
    body = make_body(dict(fine.shape))
    return jax.shard_map(body, mesh=fine, in_specs=in_specs, out_specs=out_specs, check_vma=False)
```

```python
import jax
import jax.numpy as jnp
from jax import lax
from jax.sharding import Mesh
from jax.sharding import PartitionSpec as P

EXACT = lax.Precision.HIGHEST
DEV = ("z", "x", "core")
LINE = ("z", "core")


def mm(left, right):
    return jnp.dot(left, right, precision=EXACT)


def mmt(left, right):
    return jnp.einsum("rn,mn->rm", left, right, precision=EXACT)


def swap(chunks, axes):
    return lax.all_to_all(chunks, axes, 0, 0, tiled=True)


def spread(values, axes, count):
    return swap(jnp.broadcast_to(values[None], (count,) + values.shape), axes)


def reduce_over(values, axes, count):
    return jnp.sum(spread(values, axes, count), 0)


def fold(values, folds):
    rows, width = values.shape
    tall = rows // folds
    return values.reshape(folds, tall, width).transpose(1, 0, 2).reshape(tall, folds * width)


def unfold(values, folds):
    tall, width = values.shape
    thin = width // folds
    return values.reshape(tall, folds, thin).transpose(1, 0, 2).reshape(folds * tall, thin)


def make_body(sizes):
    n_grp, n_z = sizes["grp"], sizes["z"]
    n_x, n_core = sizes["x"], sizes["core"]
    n_dev = n_z * n_x * n_core

    def body(
        leaf_right,
        leaf_inverse,
        leaf_link,
        leaf_front,
        parents,
        front_rows,
        live_blocks,
        front_right,
        front_inverse,
        front_couple,
        root_right,
        root_inverse,
        root_couple,
    ):
        rows = leaf_right.shape[0]
        width = leaf_inverse.shape[1]
        front_order = front_inverse.shape[1]
        n_front = front_order // width
        share = front_inverse.shape[0]
        part = root_inverse.shape[2]
        live = live_blocks[0]

        with jax.named_scope("gather_x"):
            chain = jnp.concatenate([root_inverse, root_couple], 0)
            chain = spread(chain, "x", n_x).transpose(1, 0, 2, 3).reshape(3, n_x * share, part)
        couple = front_couple.reshape(share, 2, n_z, n_x, n_core, share)
        couple = couple.transpose(0, 1, 2, 4, 3, 5).reshape(share, 2 * front_order)

        def dev_sum(natural):
            chunks = natural.reshape(4, rows // 4, n_dev, share).transpose(2, 1, 0, 3)
            return unfold(jnp.sum(swap(chunks.reshape(n_dev, rows // 4, 4 * share), DEV), 0), 4)

        def dev_columns(values):
            chunks = spread(fold(values, 4), DEV, n_dev).reshape(n_dev, rows // 4, 4, share)
            return chunks.transpose(2, 1, 0, 3).reshape(rows, n_dev * share)

        has_parent = parents[0] < live
        right0, right1 = leaf_right[:, :width], leaf_right[:, width:]
        solved0 = jnp.where(live > 0, mm(right0, leaf_inverse[0]), 0.0)
        lifted = jnp.where(has_parent, mm(solved0, leaf_link[0]), 0.0)
        solved1 = jnp.where(live > 1, mm(right1 - lifted, leaf_inverse[1]), 0.0)
        given0, given1 = mm(solved0, leaf_front[0]), mm(solved1, leaf_front[1])
        slots = jnp.arange(n_front, dtype=jnp.int32)[None, :, None]
        placed = jnp.where(slots == front_rows[0], given0[:, None, :], 0.0) + jnp.where(
            slots == front_rows[1], given1[:, None, :], 0.0
        )
        placed, chain = lax.optimization_barrier((placed, chain))
        with jax.named_scope("gather_grp"):
            chain = lax.all_gather(chain, "grp", axis=0, tiled=False)
        with jax.named_scope("sum_u"):
            update = dev_sum(placed.reshape(rows, front_order))
        with jax.named_scope("sum_y"):
            y_own = dev_sum(mm(front_right - update, front_inverse))

        place = (lax.axis_index("z") * n_core + lax.axis_index("core")) * n_x + lax.axis_index("x")
        spots = place * share + jnp.arange(share, dtype=jnp.int32)
        spots = jnp.concatenate([spots, front_order + spots])[:, None]
        picks = spots == jnp.arange(2 * front_order, dtype=jnp.int32)[None, :]
        picks = jnp.where(picks & (lax.axis_index("grp") == 0), 1.0, 0.0).astype(jnp.float32)
        fed = jnp.concatenate([-y_own, root_right[:, 0], root_right[:, 1]], 1)
        given = mm(fed, jnp.concatenate([couple, picks], 0))
        chunks = given.reshape(n_x, n_grp, 2, n_z, n_core, n_x * share).transpose(3, 0, 4, 1, 2, 5)
        with jax.named_scope("sum_v"):
            given = jnp.sum(swap(chunks.reshape(n_dev, n_grp, 2 * n_x * share), DEV), 0)
        given, chain = lax.optimization_barrier((given, chain))
        with jax.named_scope("sum_g"):
            given = reduce_over(given, "grp", n_grp)
        mine = jnp.arange(n_grp, dtype=jnp.int32)[:, None] == lax.axis_index("grp")
        given = jnp.sum(jnp.where(mine, given, 0.0), 0, keepdims=True)

        w_low, w_high, link = chain[:, 0], chain[:, 1], chain[:, 2]

        def across(values, matrix):
            wide = jnp.einsum("rk,gkc->rgc", values, matrix, precision=EXACT)
            return reduce_over(wide.reshape(n_grp, part), LINE, n_z * n_core)

        def along(values, matrix):
            return jnp.einsum("gc,gkc->k", values, matrix, precision=EXACT)[None, :]

        low, high = given[:, : n_x * share], given[:, n_x * share :]
        y_high = across(high, w_high)
        low = low - along(y_high, link)
        x_low = along(across(low, w_low), w_low)
        x_high = along(y_high - across(x_low, link), w_high)

        with jax.named_scope("root_g"):
            both = jnp.concatenate([x_low, x_high], 1)
            whole = spread(both, "grp", n_grp).reshape(n_grp, 2 * n_x * share)
        with jax.named_scope("root_d"):
            whole = spread(whole, DEV, n_dev)
        whole = whole.reshape(n_z, n_x, n_core, n_grp, 2, n_x * share).transpose(1, 3, 4, 0, 2, 5)
        whole = whole.reshape(rows, 2 * front_order)
        rest = y_own - mmt(whole, couple)
        rest = dev_columns(rest)
        front_solution = dev_columns(mmt(rest, front_inverse))

        def back(solved, block):
            picked = lax.dynamic_slice(front_solution, (0, front_rows[block] * width), (rows, width))
            return solved - mmt(picked, leaf_front[block])

        base0, base1 = back(solved0, 0), back(solved1, 1)
        leaf1 = jnp.where(live > 1, mmt(base1, leaf_inverse[1]), 0.0)
        carried = jnp.where(has_parent, mmt(leaf1, leaf_link[0]), 0.0)
        leaf0 = jnp.where(live > 0, mmt(base0 - carried, leaf_inverse[0]), 0.0)
        leaf_solution = jnp.concatenate([leaf0, leaf1], 1)
        root = whole.reshape(rows, 2, front_order)
        root = lax.dynamic_slice(root, (0, 0, place * share), (rows, 2, share))
        return leaf_solution, front_solution, root

    return body


def solution(mesh):
    n_grp, n_dev = mesh.shape["grp"], mesh.shape["dev"]
    fine = Mesh(mesh.devices.reshape(n_grp, n_dev // 8, 4, 2), ("grp", "z", "x", "core"))
    every = ("grp",) + DEV
    in_specs = (
        P(None, every),
        P(every, None, None),
        P(every, None, None),
        P(every, None, None),
        P(every),
        P(every),
        P(every),
        P(None, every),
        P(every, None),
        P(every, None),
        P(None, None, DEV),
        P(None, DEV, "grp"),
        P(None, DEV, "grp"),
    )
    out_specs = (P(None, every), P(None, "grp"), P(None, None, DEV))
    body = make_body(dict(fine.shape))
    return jax.shard_map(body, mesh=fine, in_specs=in_specs, out_specs=out_specs, check_vma=False)
```

```python
import jax
import jax.numpy as jnp
from jax import lax
from jax.sharding import Mesh
from jax.sharding import PartitionSpec as P

EXACT = lax.Precision.HIGHEST
DEV = ("z", "x", "core")


def mm(left, right):
    return jnp.dot(left, right, precision=EXACT)


def mmt(left, right):
    return jnp.einsum("rn,mn->rm", left, right, precision=EXACT)


def swap(chunks, axes):
    return lax.all_to_all(chunks, axes, 0, 0, tiled=True)


def spread(values, axes, count):
    return swap(jnp.broadcast_to(values[None], (count,) + values.shape), axes)


def reduce_over(values, axes, count):
    return jnp.sum(spread(values, axes, count), 0)


def fold(values, folds):
    rows, width = values.shape
    tall = rows // folds
    return values.reshape(folds, tall, width).transpose(1, 0, 2).reshape(tall, folds * width)


def unfold(values, folds):
    tall, width = values.shape
    thin = width // folds
    return values.reshape(tall, folds, thin).transpose(1, 0, 2).reshape(folds * tall, thin)


def make_body(sizes):
    n_grp, n_z = sizes["grp"], sizes["z"]
    n_x = sizes["x"]
    n_near = n_x * sizes["core"]
    n_dev = n_z * n_near

    def body(
        leaf_right,
        leaf_inverse,
        leaf_link,
        leaf_front,
        parents,
        front_rows,
        live_blocks,
        front_right,
        front_inverse,
        front_couple,
        root_right,
        root_inverse,
        root_couple,
    ):
        rows = leaf_right.shape[0]
        width = leaf_inverse.shape[1]
        front_order = front_inverse.shape[1]
        n_front = front_order // width
        share = front_inverse.shape[0]
        part = root_inverse.shape[2]
        few = rows // n_near
        live = live_blocks[0]
        my_dev = lax.axis_index(DEV)

        chain = jnp.concatenate([root_inverse, root_couple], 0)
        chain = spread(chain, "x", n_x)

        def dev_sum(natural):
            chunks = natural.reshape(4, rows // 4, n_dev, share).transpose(2, 1, 0, 3)
            return unfold(jnp.sum(swap(chunks.reshape(n_dev, rows // 4, 4 * share), DEV), 0), 4)

        def dev_columns(values):
            chunks = spread(fold(values, 4), DEV, n_dev).reshape(n_dev, rows // 4, 4, share)
            return chunks.transpose(2, 1, 0, 3).reshape(rows, n_dev * share)

        has_parent = parents[0] < live
        right0, right1 = leaf_right[:, :width], leaf_right[:, width:]
        solved0 = jnp.where(live > 0, mm(right0, leaf_inverse[0]), 0.0)
        lifted = jnp.where(has_parent, mm(solved0, leaf_link[0]), 0.0)
        solved1 = jnp.where(live > 1, mm(right1 - lifted, leaf_inverse[1]), 0.0)
        given0, given1 = mm(solved0, leaf_front[0]), mm(solved1, leaf_front[1])
        slots = jnp.arange(n_front, dtype=jnp.int32)[None, :, None]
        placed = jnp.where(slots == front_rows[0], given0[:, None, :], 0.0) + jnp.where(
            slots == front_rows[1], given1[:, None, :], 0.0
        )
        placed, chain = lax.optimization_barrier((placed, chain))
        chain = lax.all_gather(chain, "core", axis=0).transpose(2, 1, 0, 3, 4)
        chain = chain.reshape(3, n_near * share, part)
        placed, chain = lax.optimization_barrier((placed, chain))
        w_low, w_high, link = chain[0], chain[1], chain[2]
        start = front_right - dev_sum(placed.reshape(rows, front_order))
        y_own = dev_sum(mm(start, front_inverse))

        spots = my_dev * share + jnp.arange(share, dtype=jnp.int32)
        spots = jnp.concatenate([spots, front_order + spots])[:, None]
        picks = spots == jnp.arange(2 * front_order, dtype=jnp.int32)[None, :]
        picks = jnp.where(picks & (lax.axis_index("grp") == 0), 1.0, 0.0).astype(jnp.float32)
        fed = jnp.concatenate([-y_own, root_right[:, 0], root_right[:, 1]], 1)
        given = mm(fed, jnp.concatenate([front_couple, picks], 0))
        chunks = given.reshape(n_near, few, 2, n_z, part).transpose(3, 0, 2, 1, 4)
        given = jnp.sum(swap(chunks.reshape(n_dev, 2 * few, part), DEV), 0)
        given = reduce_over(given, "grp", n_grp)

        low, high = given[:few], given[few:]
        y_high = reduce_over(mm(high, w_high), "z", n_z)
        low = low - reduce_over(mmt(y_high, link), "grp", n_grp)
        y_low = reduce_over(mm(low, w_low), "z", n_z)
        x_low = reduce_over(mmt(y_low, w_low), "grp", n_grp)
        y_high = y_high - reduce_over(mm(x_low, link), "z", n_z)
        x_high = reduce_over(mmt(y_high, w_high), "grp", n_grp)

        whole = spread(jnp.concatenate([x_low, x_high], 0), DEV, n_dev)
        whole = whole.reshape(n_z, n_near, 2, few, part).transpose(1, 3, 2, 0, 4)
        whole = whole.reshape(rows, 2 * front_order)
        rest = dev_columns(y_own - mmt(whole, front_couple))
        front_solution = dev_columns(mmt(rest, front_inverse))

        def back(solved, block):
            picked = lax.dynamic_slice(front_solution, (0, front_rows[block] * width), (rows, width))
            return solved - mmt(picked, leaf_front[block])

        base0, base1 = back(solved0, 0), back(solved1, 1)
        leaf1 = jnp.where(live > 1, mmt(base1, leaf_inverse[1]), 0.0)
        carried = jnp.where(has_parent, mmt(leaf1, leaf_link[0]), 0.0)
        leaf0 = jnp.where(live > 0, mmt(base0 - carried, leaf_inverse[0]), 0.0)
        leaf_solution = jnp.concatenate([leaf0, leaf1], 1)
        root = whole.reshape(rows, 2, front_order)
        root = lax.dynamic_slice(root, (0, 0, my_dev * share), (rows, 2, share))
        return leaf_solution, front_solution, root

    return body


def solution(mesh):
    n_grp, n_dev = mesh.shape["grp"], mesh.shape["dev"]
    fine = Mesh(mesh.devices.reshape(n_grp, n_dev // 8, 4, 2), ("grp", "z", "x", "core"))
    every = ("grp",) + DEV
    in_specs = (
        P(None, every),
        P(every, None, None),
        P(every, None, None),
        P(every, None, None),
        P(every),
        P(every),
        P(every),
        P(None, every),
        P(every, None),
        P(every, None),
        P(None, None, DEV),
        P(None, DEV, "grp"),
        P(None, DEV, "grp"),
    )
    out_specs = (P(None, every), P(None, "grp"), P(None, None, DEV))
    body = make_body(dict(fine.shape))
    return jax.shard_map(body, mesh=fine, in_specs=in_specs, out_specs=out_specs, check_vma=False)
```

```python
import jax
import jax.numpy as jnp
from jax import lax
from jax.sharding import Mesh
from jax.sharding import PartitionSpec as P


EXACT = lax.Precision.HIGHEST
DEV = ("z", "x", "core")
LINE = ("z", "core")


def mm(left, right):
    return jnp.dot(left, right, precision=EXACT)


def mmt(left, right):
    return jnp.einsum("rn,mn->rm", left, right, precision=EXACT)


def swap(chunks, axes):
    return lax.all_to_all(chunks, axes, 0, 0, tiled=True)


def spread(values, axes, count):
    return swap(jnp.broadcast_to(values[None], (count,) + values.shape), axes)


def reduce_over(values, axes, count):
    return jnp.sum(spread(values, axes, count), 0)


def make_body(sizes):
    n_grp, n_z = sizes["grp"], sizes["z"]
    n_x, n_core = sizes["x"], sizes["core"]
    n_line = n_z * n_core
    n_dev = n_line * n_x

    def body(
        leaf_right,
        leaf_inverse,
        leaf_link,
        leaf_front,
        parents,
        front_rows,
        live_blocks,
        front_right,
        front_inverse,
        front_couple,
        root_right,
        root_inverse,
        root_couple,
    ):
        rows = leaf_right.shape[0]
        width = leaf_inverse.shape[1]
        front_order = front_inverse.shape[1]
        n_front = front_order // width
        share = front_inverse.shape[0]
        part = root_inverse.shape[2]
        some, few = rows // n_x, rows // (n_x * n_core)
        live = live_blocks[0]
        my_z, my_x, my_core = (lax.axis_index(name) for name in DEV)

        def from_right(values, step):
            pairs = [((i + step) % n_x, i) for i in range(n_x)]
            return lax.ppermute(values, "x", pairs)

        def turn(values, steps):
            return lax.dynamic_slice_in_dim(
                jnp.concatenate([values, values], 1), steps * share, n_x * share, 1
            )

        small = (root_inverse, root_couple, root_right, front_right)
        bundle = jnp.concatenate([item.reshape(-1, part) for item in small], 0)
        tall = bundle.shape[0]
        bundle = jnp.pad(bundle, ((0, -tall % 8), (0, 0)))
        bundle = spread(bundle, "x", n_x)

        has_parent = parents[0] < live
        right0, right1 = leaf_right[:, :width], leaf_right[:, width:]
        solved0 = jnp.where(live > 0, mm(right0, leaf_inverse[0]), 0.0)
        lifted = jnp.where(has_parent, mm(solved0, leaf_link[0]), 0.0)
        solved1 = jnp.where(live > 1, mm(right1 - lifted, leaf_inverse[1]), 0.0)
        given0, given1 = mm(solved0, leaf_front[0]), mm(solved1, leaf_front[1])
        slots = jnp.arange(n_front, dtype=jnp.int32)[None, :, None]
        placed = jnp.where(slots == front_rows[0], given0[:, None, :], 0.0) + jnp.where(
            slots == front_rows[1], given1[:, None, :], 0.0
        )
        placed, bundle = lax.optimization_barrier((placed, bundle))
        bundle = lax.all_gather(bundle, "core", axis=0)
        placed, bundle = lax.optimization_barrier((placed, bundle))
        chain = bundle[:, :, : 3 * share].reshape(n_core, n_x, 3, share, part)
        chain = chain.transpose(2, 1, 0, 3, 4).reshape(3, n_x * n_core * share, part)
        w_low, w_high, link = chain[0], chain[1], chain[2]
        n_root = root_right.size // part
        sides = bundle[:, :, 3 * share : 3 * share + n_root]
        sides = lax.dynamic_index_in_dim(sides, my_x * n_core + my_core, 2, False)
        sides = sides.reshape(n_core, n_x, few, 2, share).transpose(3, 2, 1, 0, 4)
        sides = sides.reshape(2 * few, part)
        fronts = bundle[:, :, 3 * share + n_root : tall]
        fronts = lax.dynamic_index_in_dim(fronts, my_core, 0, False)
        fronts = lax.dynamic_index_in_dim(fronts, my_x, 1, False)
        fronts = fronts.reshape(n_x, some, share).transpose(1, 0, 2).reshape(some, n_x * share)

        inverses, couples = [front_inverse], [front_couple]
        for step in (1, 3, 2):
            inverses.append(from_right(front_inverse, step))
        for step in (1, 3, 2):
            couples.append(from_right(front_couple, step))
        order = (0, 1, 3, 2)
        inverses = [inverses[order.index(step)] for step in range(n_x)]
        couples = [couples[order.index(step)] for step in range(n_x)]

        def across(values, pieces):
            values = turn(values, my_x)
            return sum(
                mm(values[:, step * share : (step + 1) * share], piece)
                for step, piece in enumerate(pieces)
            )

        def along(values, pieces):
            found = jnp.concatenate([mmt(values, piece) for piece in pieces], 1)
            return turn(found, (n_x - my_x) % n_x)

        chunks = placed.reshape(n_x, some, n_z, n_x, n_core, share).transpose(2, 0, 4, 1, 3, 5)
        update = jnp.sum(swap(chunks.reshape(n_dev, some, n_x * share), DEV), 0)
        terms = across(fronts - update, inverses)
        chunks = terms.reshape(some, n_z, n_x, n_core, share).transpose(1, 3, 0, 2, 4)
        y_front = jnp.sum(swap(chunks.reshape(n_line, some, n_x * share), LINE), 0)
        raised = across(y_front, couples).reshape(n_core, few, 2, n_z, part)
        chunks = raised.transpose(3, 0, 2, 1, 4).reshape(n_line, 2 * few, part)
        raised = jnp.sum(swap(chunks, LINE), 0)
        given = sides - reduce_over(raised, "grp", n_grp)

        low, high = given[:few], given[few:]
        y_high = reduce_over(mm(high, w_high), "z", n_z)
        low = low - reduce_over(mmt(y_high, link), "grp", n_grp)
        y_low = reduce_over(mm(low, w_low), "z", n_z)
        x_low = reduce_over(mmt(y_low, w_low), "grp", n_grp)
        y_high = y_high - reduce_over(mm(x_low, link), "z", n_z)
        x_high = reduce_over(mmt(y_high, w_high), "grp", n_grp)

        whole = spread(jnp.concatenate([x_low, x_high], 0), LINE, n_line)
        whole = whole.reshape(n_z, n_core, 2, few, part).transpose(1, 3, 2, 0, 4)
        whole = whole.reshape(some, 2 * front_order)
        rest = spread(y_front - along(whole, couples), LINE, n_line)
        rest = rest.reshape(n_z, n_core, some, n_x, share).transpose(2, 0, 3, 1, 4)
        found = along(rest.reshape(some, front_order), inverses)
        root = whole.reshape(some, 2, n_z * n_x * n_core, share).transpose(2, 0, 1, 3)
        root = jnp.pad(root.reshape(n_dev, some, 2 * share), ((0, 0), (0, 0), (0, 2 * share)))
        found = jnp.broadcast_to(found[None], (n_dev, some, n_x * share))
        mixed = swap(jnp.concatenate([found, root], 2), DEV)
        front_solution = mixed[:, :, : n_x * share].reshape(n_z, n_x, n_core, some, n_x, share)
        front_solution = front_solution.transpose(1, 3, 0, 4, 2, 5).reshape(rows, front_order)
        root = mixed[:, :, n_x * share : (n_x + 2) * share]
        root = root.reshape(n_z, n_x, n_core, some, 2 * share)
        root = lax.dynamic_index_in_dim(root, my_z, 0, False)
        root = lax.dynamic_index_in_dim(root, my_core, 1, False).reshape(rows, 2, share)

        def back(solved, block):
            picked = lax.dynamic_slice(front_solution, (0, front_rows[block] * width), (rows, width))
            return solved - mmt(picked, leaf_front[block])

        base0, base1 = back(solved0, 0), back(solved1, 1)
        leaf1 = jnp.where(live > 1, mmt(base1, leaf_inverse[1]), 0.0)
        carried = jnp.where(has_parent, mmt(leaf1, leaf_link[0]), 0.0)
        leaf0 = jnp.where(live > 0, mmt(base0 - carried, leaf_inverse[0]), 0.0)
        leaf_solution = jnp.concatenate([leaf0, leaf1], 1)
        return leaf_solution, front_solution, root

    return body


def solution(mesh):
    n_grp, n_dev = mesh.shape["grp"], mesh.shape["dev"]
    fine = Mesh(mesh.devices.reshape(n_grp, n_dev // 8, 4, 2), ("grp", "z", "x", "core"))
    every = ("grp",) + DEV
    in_specs = (
        P(None, every),
        P(every, None, None),
        P(every, None, None),
        P(every, None, None),
        P(every),
        P(every),
        P(every),
        P(None, every),
        P(every, None),
        P(every, None),
        P(None, None, DEV),
        P(None, DEV, "grp"),
        P(None, DEV, "grp"),
    )
    out_specs = (P(None, every), P(None, "grp"), P(None, None, DEV))
    inner = make_body(dict(fine.shape))

    return jax.shard_map(inner, mesh=fine, in_specs=in_specs, out_specs=out_specs, check_vma=False)
```

```python
import jax
import jax.numpy as jnp
from jax import lax
from jax.sharding import Mesh
from jax.sharding import PartitionSpec as P


EXACT = lax.Precision.HIGHEST
DEV = ("z", "x", "core")
LINE = ("z", "core")


def mm(left, right):
    return jnp.dot(left, right, precision=EXACT)


def mmt(left, right):
    return jnp.einsum("rn,mn->rm", left, right, precision=EXACT)


def swap(chunks, axes):
    return lax.all_to_all(chunks, axes, 0, 0, tiled=True)


def spread(values, axes, count):
    return swap(jnp.broadcast_to(values[None], (count,) + values.shape), axes)


def reduce_over(values, axes, count):
    return jnp.sum(spread(values, axes, count), 0)


def unfold(values, folds):
    tall, width = values.shape
    thin = width // folds
    return values.reshape(tall, folds, thin).transpose(1, 0, 2).reshape(folds * tall, thin)


def make_body(sizes):
    n_grp, n_z = sizes["grp"], sizes["z"]
    n_x, n_core = sizes["x"], sizes["core"]
    n_near, n_line = n_x * n_core, n_z * n_core
    n_dev = n_z * n_near

    def body(
        leaf_right,
        leaf_inverse,
        leaf_link,
        leaf_front,
        parents,
        front_rows,
        live_blocks,
        front_right,
        front_inverse,
        front_couple,
        root_right,
        root_inverse,
        root_couple,
    ):
        rows = leaf_right.shape[0]
        width = leaf_inverse.shape[1]
        front_order = front_inverse.shape[1]
        n_front = front_order // width
        share = front_inverse.shape[0]
        part = root_inverse.shape[2]
        few = rows // n_near
        live = live_blocks[0]
        my_dev = lax.axis_index(DEV)
        my_z, my_x, my_core = (lax.axis_index(name) for name in DEV)
        some = rows // n_x

        def from_right(values, step):
            pairs = [((i + step) % n_x, i) for i in range(n_x)]
            return lax.ppermute(values, "x", pairs)

        def turn(values, axis, steps):
            size = values.shape[axis]
            doubled = jnp.concatenate([values, values], axis)
            return lax.dynamic_slice_in_dim(doubled, steps * (size // n_x), size, axis)

        inverses = [front_inverse] + [from_right(front_inverse, i) for i in range(1, n_x)]
        couples = [front_couple] + [from_right(front_couple, i) for i in range(1, n_x)]

        def along(values, pieces):
            return jnp.concatenate([mmt(values, piece) for piece in pieces], 1)

        chain = jnp.concatenate([root_inverse, root_couple], 0)
        chain = spread(chain, "x", n_x)

        def dev_sum(natural):
            chunks = natural.reshape(4, rows // 4, n_dev, share).transpose(2, 1, 0, 3)
            return unfold(jnp.sum(swap(chunks.reshape(n_dev, rows // 4, 4 * share), DEV), 0), 4)

        has_parent = parents[0] < live
        right0, right1 = leaf_right[:, :width], leaf_right[:, width:]
        solved0 = jnp.where(live > 0, mm(right0, leaf_inverse[0]), 0.0)
        lifted = jnp.where(has_parent, mm(solved0, leaf_link[0]), 0.0)
        solved1 = jnp.where(live > 1, mm(right1 - lifted, leaf_inverse[1]), 0.0)
        given0, given1 = mm(solved0, leaf_front[0]), mm(solved1, leaf_front[1])
        slots = jnp.arange(n_front, dtype=jnp.int32)[None, :, None]
        placed = jnp.where(slots == front_rows[0], given0[:, None, :], 0.0) + jnp.where(
            slots == front_rows[1], given1[:, None, :], 0.0
        )
        placed, chain = lax.optimization_barrier((placed, chain))
        chain = lax.all_gather(chain, "core", axis=0).transpose(2, 1, 0, 3, 4)
        chain = chain.reshape(3, n_near * share, part)
        placed, chain = lax.optimization_barrier((placed, chain))
        w_low, w_high, link = chain[0], chain[1], chain[2]
        start = front_right - dev_sum(placed.reshape(rows, front_order))
        y_own = dev_sum(mm(start, front_inverse))
        y_some = []
        for step in range(n_x):
            spot = (my_x + n_x - step) % n_x * some
            piece = lax.dynamic_slice_in_dim(y_own, spot, some, 0)
            y_some.append(from_right(piece, step) if step else piece)
        y_some = jnp.concatenate(y_some, 1)

        spots = my_dev * share + jnp.arange(share, dtype=jnp.int32)
        spots = jnp.concatenate([spots, front_order + spots])[:, None]
        picks = spots == jnp.arange(2 * front_order, dtype=jnp.int32)[None, :]
        picks = jnp.where(picks & (lax.axis_index("grp") == 0), 1.0, 0.0).astype(jnp.float32)
        fed = jnp.concatenate([-y_own, root_right[:, 0], root_right[:, 1]], 1)
        given = mm(fed, jnp.concatenate([front_couple, picks], 0))
        chunks = given.reshape(n_near, few, 2, n_z, part).transpose(3, 0, 2, 1, 4)
        given = jnp.sum(swap(chunks.reshape(n_dev, 2 * few, part), DEV), 0)
        given = reduce_over(given, "grp", n_grp)

        low, high = given[:few], given[few:]
        y_high = reduce_over(mm(high, w_high), "z", n_z)
        low = low - reduce_over(mmt(y_high, link), "grp", n_grp)
        y_low = reduce_over(mm(low, w_low), "z", n_z)
        x_low = reduce_over(mmt(y_low, w_low), "grp", n_grp)
        y_high = y_high - reduce_over(mm(x_low, link), "z", n_z)
        x_high = reduce_over(mmt(y_high, w_high), "grp", n_grp)

        whole = spread(jnp.concatenate([x_low, x_high], 0), LINE, n_line)
        whole = whole.reshape(n_z, n_core, 2, few, part).transpose(1, 3, 2, 0, 4)
        whole = whole.reshape(some, 2 * front_order)
        rest = turn(y_some - along(whole, couples), 1, (n_x - my_x) % n_x)
        rest = spread(rest, LINE, n_line)
        rest = rest.reshape(n_z, n_core, some, n_x, share).transpose(2, 0, 3, 1, 4)
        found = along(rest.reshape(some, front_order), inverses)
        found = turn(found, 1, (n_x - my_x) % n_x)
        found = spread(found, DEV, n_dev).reshape(n_z, n_x, n_core, some, n_x, share)
        front_solution = found.transpose(1, 3, 0, 4, 2, 5).reshape(rows, front_order)
        root = []
        for step in range(n_x):
            spot = my_z * part + (my_x + n_x - step) % n_x * (n_core * share) + my_core * share
            pieces = [
                lax.dynamic_slice_in_dim(whole, spot + level * front_order, share, 1)
                for level in range(2)
            ]
            piece = jnp.concatenate(pieces, 1)
            root.append(from_right(piece, step) if step else piece)
        root = turn(jnp.concatenate(root, 0), 0, (n_x - my_x) % n_x).reshape(rows, 2, share)

        def back(solved, block):
            picked = lax.dynamic_slice(front_solution, (0, front_rows[block] * width), (rows, width))
            return solved - mmt(picked, leaf_front[block])

        base0, base1 = back(solved0, 0), back(solved1, 1)
        leaf1 = jnp.where(live > 1, mmt(base1, leaf_inverse[1]), 0.0)
        carried = jnp.where(has_parent, mmt(leaf1, leaf_link[0]), 0.0)
        leaf0 = jnp.where(live > 0, mmt(base0 - carried, leaf_inverse[0]), 0.0)
        leaf_solution = jnp.concatenate([leaf0, leaf1], 1)
        return leaf_solution, front_solution, root

    return body


def solution(mesh):
    n_grp, n_dev = mesh.shape["grp"], mesh.shape["dev"]
    fine = Mesh(mesh.devices.reshape(n_grp, n_dev // 8, 4, 2), ("grp", "z", "x", "core"))
    every = ("grp",) + DEV
    in_specs = (
        P(None, every),
        P(every, None, None),
        P(every, None, None),
        P(every, None, None),
        P(every),
        P(every),
        P(every),
        P(None, every),
        P(every, None),
        P(every, None),
        P(None, None, DEV),
        P(None, DEV, "grp"),
        P(None, DEV, "grp"),
    )
    out_specs = (P(None, every), P(None, "grp"), P(None, None, DEV))
    inner = make_body(dict(fine.shape))

    return jax.shard_map(inner, mesh=fine, in_specs=in_specs, out_specs=out_specs, check_vma=False)
```

```python
import jax
import jax.numpy as jnp
from jax import lax
from jax.sharding import Mesh
from jax.sharding import PartitionSpec as P


EXACT = lax.Precision.HIGHEST
DEV = ("z", "x", "core")
LINE = ("z", "core")


def mm(left, right):
    return jnp.dot(left, right, precision=EXACT)


def mmt(left, right):
    return jnp.einsum("rn,mn->rm", left, right, precision=EXACT)


def swap(chunks, axes):
    return lax.all_to_all(chunks, axes, 0, 0, tiled=True)


def spread(values, axes, count):
    return swap(jnp.broadcast_to(values[None], (count,) + values.shape), axes)


def reduce_over(values, axes, count):
    return jnp.sum(spread(values, axes, count), 0)


def unfold(values, folds):
    tall, width = values.shape
    thin = width // folds
    return values.reshape(tall, folds, thin).transpose(1, 0, 2).reshape(folds * tall, thin)


def make_body(sizes):
    n_grp, n_z = sizes["grp"], sizes["z"]
    n_x, n_core = sizes["x"], sizes["core"]
    n_near, n_line = n_x * n_core, n_z * n_core
    n_dev = n_z * n_near

    def body(
        leaf_right,
        leaf_inverse,
        leaf_link,
        leaf_front,
        parents,
        front_rows,
        live_blocks,
        front_right,
        front_inverse,
        front_couple,
        root_right,
        root_inverse,
        root_couple,
    ):
        rows = leaf_right.shape[0]
        width = leaf_inverse.shape[1]
        front_order = front_inverse.shape[1]
        n_front = front_order // width
        share = front_inverse.shape[0]
        part = root_inverse.shape[2]
        few = rows // n_near
        live = live_blocks[0]
        my_dev = lax.axis_index(DEV)
        my_z, my_x, my_core = (lax.axis_index(name) for name in DEV)
        some = rows // n_x

        def from_right(values, step):
            pairs = [((i + step) % n_x, i) for i in range(n_x)]
            return lax.ppermute(values, "x", pairs)

        def turn(values, axis, steps):
            size = values.shape[axis]
            doubled = jnp.concatenate([values, values], axis)
            return lax.dynamic_slice_in_dim(doubled, steps * (size // n_x), size, axis)

        def from_all(values):
            return [values] + [from_right(values, step) for step in range(1, n_x)]

        chain = from_all(jnp.concatenate([root_inverse, root_couple], 0))
        chain = lax.all_gather(jnp.stack(chain, 0), "core", axis=0)
        chain = chain.transpose(2, 1, 0, 3, 4).reshape(3, n_near * share, part)
        w_low, w_high, link = chain[0], chain[1], chain[2]
        inverses = from_all(front_inverse)

        def dev_sum(natural):
            chunks = natural.reshape(4, rows // 4, n_dev, share).transpose(2, 1, 0, 3)
            return unfold(jnp.sum(swap(chunks.reshape(n_dev, rows // 4, 4 * share), DEV), 0), 4)

        has_parent = parents[0] < live
        right0, right1 = leaf_right[:, :width], leaf_right[:, width:]
        solved0 = jnp.where(live > 0, mm(right0, leaf_inverse[0]), 0.0)
        lifted = jnp.where(has_parent, mm(solved0, leaf_link[0]), 0.0)
        solved1 = jnp.where(live > 1, mm(right1 - lifted, leaf_inverse[1]), 0.0)
        given0, given1 = mm(solved0, leaf_front[0]), mm(solved1, leaf_front[1])
        slots = jnp.arange(n_front, dtype=jnp.int32)[None, :, None]
        placed = jnp.where(slots == front_rows[0], given0[:, None, :], 0.0) + jnp.where(
            slots == front_rows[1], given1[:, None, :], 0.0
        )
        start = front_right - dev_sum(placed.reshape(rows, front_order))
        y_own = dev_sum(mm(start, front_inverse))
        side = jnp.pad(y_own, ((0, 0), (0, width - share)))
        couples = from_all(jnp.concatenate([front_couple, side], 1))

        spots = my_dev * share + jnp.arange(share, dtype=jnp.int32)
        spots = jnp.concatenate([spots, front_order + spots])[:, None]
        picks = spots == jnp.arange(2 * front_order, dtype=jnp.int32)[None, :]
        picks = jnp.where(picks & (lax.axis_index("grp") == 0), 1.0, 0.0).astype(jnp.float32)
        fed = jnp.concatenate([-y_own, root_right[:, 0], root_right[:, 1]], 1)
        given = mm(fed, jnp.concatenate([front_couple, picks], 0))
        chunks = given.reshape(n_near, few, 2, n_z, part).transpose(3, 0, 2, 1, 4)
        given = jnp.sum(swap(chunks.reshape(n_dev, 2 * few, part), DEV), 0)
        given = reduce_over(given, "grp", n_grp)

        given = turn(given, 1, my_x)
        low, high = given[:few], given[few:]
        y_high = reduce_over(mm(high, w_high), "z", n_z)
        low = low - reduce_over(mmt(y_high, link), "grp", n_grp)
        y_low = reduce_over(mm(low, w_low), "z", n_z)
        x_low = reduce_over(mmt(y_low, w_low), "grp", n_grp)
        joined = jnp.concatenate([piece[:, : 2 * front_order] for piece in couples], 0)
        inverse = jnp.concatenate(inverses, 0)
        y_some = [
            lax.dynamic_slice_in_dim(piece[:, 2 * front_order :], my_x * some, some, 0)[:, :share]
            for piece in couples
        ]
        y_some = jnp.concatenate(y_some, 1)
        x_low, joined, inverse, y_some = lax.optimization_barrier((x_low, joined, inverse, y_some))
        y_high = y_high - reduce_over(mm(x_low, link), "z", n_z)
        x_high = reduce_over(mmt(y_high, w_high), "grp", n_grp)

        back_turn = (n_x - my_x) % n_x
        both = turn(jnp.concatenate([x_low, x_high], 0), 1, back_turn)
        whole = spread(both, LINE, n_line)
        whole = whole.reshape(n_z, n_core, 2, few, part).transpose(1, 3, 2, 0, 4)
        whole = whole.reshape(some, 2 * front_order)
        rest = turn(y_some - mmt(whole, joined), 1, back_turn)
        rest = spread(rest, LINE, n_line)
        rest = rest.reshape(n_z, n_core, some, n_x, share).transpose(2, 0, 3, 1, 4)
        found = turn(mmt(rest.reshape(some, front_order), inverse), 1, back_turn)
        found = spread(found, DEV, n_dev).reshape(n_z, n_x, n_core, some, n_x, share)
        front_solution = found.transpose(1, 3, 0, 4, 2, 5).reshape(rows, front_order)
        root = []
        for step in range(n_x):
            spot = my_z * part + (my_x + n_x - step) % n_x * (n_core * share) + my_core * share
            pieces = [
                lax.dynamic_slice_in_dim(whole, spot + level * front_order, share, 1)
                for level in range(2)
            ]
            piece = jnp.concatenate(pieces, 1)
            root.append(from_right(piece, step) if step else piece)
        root = turn(jnp.concatenate(root, 0), 0, back_turn).reshape(rows, 2, share)

        def back(solved, block):
            picked = lax.dynamic_slice(front_solution, (0, front_rows[block] * width), (rows, width))
            return solved - mmt(picked, leaf_front[block])

        base0, base1 = back(solved0, 0), back(solved1, 1)
        leaf1 = jnp.where(live > 1, mmt(base1, leaf_inverse[1]), 0.0)
        carried = jnp.where(has_parent, mmt(leaf1, leaf_link[0]), 0.0)
        leaf0 = jnp.where(live > 0, mmt(base0 - carried, leaf_inverse[0]), 0.0)
        leaf_solution = jnp.concatenate([leaf0, leaf1], 1)
        return leaf_solution, front_solution, root

    return body


def solution(mesh):
    n_grp, n_dev = mesh.shape["grp"], mesh.shape["dev"]
    fine = Mesh(mesh.devices.reshape(n_grp, n_dev // 8, 4, 2), ("grp", "z", "x", "core"))
    every = ("grp",) + DEV
    in_specs = (
        P(None, every),
        P(every, None, None),
        P(every, None, None),
        P(every, None, None),
        P(every),
        P(every),
        P(every),
        P(None, every),
        P(every, None),
        P(every, None),
        P(None, None, DEV),
        P(None, DEV, "grp"),
        P(None, DEV, "grp"),
    )
    out_specs = (P(None, every), P(None, "grp"), P(None, None, DEV))
    inner = make_body(dict(fine.shape))

    return jax.shard_map(inner, mesh=fine, in_specs=in_specs, out_specs=out_specs, check_vma=False)
```

```python
import jax
import jax.numpy as jnp
from jax import lax
from jax.sharding import Mesh
from jax.sharding import PartitionSpec as P


EXACT = lax.Precision.HIGHEST
DEV = ("z", "x", "core")
LINE = ("z", "core")


def mm(left, right):
    return jnp.dot(left, right, precision=EXACT)


def mmt(left, right):
    return jnp.einsum("rn,mn->rm", left, right, precision=EXACT)


def swap(chunks, axes):
    return lax.all_to_all(chunks, axes, 0, 0, tiled=True)


def spread(values, axes, count):
    return swap(jnp.broadcast_to(values[None], (count,) + values.shape), axes)


def reduce_over(values, axes, count):
    return jnp.sum(spread(values, axes, count), 0)


def unfold(values, folds):
    tall, width = values.shape
    thin = width // folds
    return values.reshape(tall, folds, thin).transpose(1, 0, 2).reshape(folds * tall, thin)


def make_body(sizes):
    n_grp, n_z = sizes["grp"], sizes["z"]
    n_x, n_core = sizes["x"], sizes["core"]
    n_near, n_line = n_x * n_core, n_z * n_core
    n_dev = n_z * n_near

    def body(
        leaf_right,
        leaf_inverse,
        leaf_link,
        leaf_front,
        parents,
        front_rows,
        live_blocks,
        front_right,
        front_inverse,
        front_couple,
        root_right,
        root_inverse,
        root_couple,
    ):
        rows = leaf_right.shape[0]
        width = leaf_inverse.shape[1]
        front_order = front_inverse.shape[1]
        n_front = front_order // width
        share = front_inverse.shape[0]
        part = root_inverse.shape[2]
        few = rows // n_near
        live = live_blocks[0]
        my_dev = lax.axis_index(DEV)
        my_z, my_x, my_core = (lax.axis_index(name) for name in DEV)
        some = rows // n_x

        def from_right(values, step):
            pairs = [((i + step) % n_x, i) for i in range(n_x)]
            return lax.ppermute(values, "x", pairs)

        def turn(values, axis, start):
            doubled = jnp.concatenate([values, values], axis)
            return lax.dynamic_slice_in_dim(doubled, start, values.shape[axis], axis)

        def from_all(values):
            return [values] + [from_right(values, step) for step in range(1, n_x)]

        chain = from_all(jnp.concatenate([root_inverse, root_couple], 0))
        chain = lax.all_gather(jnp.stack(chain, 0), "core", axis=0)
        chain = [
            chain[:, :, item].transpose(1, 0, 2, 3).reshape(n_near * share, part)
            for item in range(3)
        ]
        w_low, w_high, link = lax.optimization_barrier(tuple(chain))
        inverses = from_all(front_inverse)

        def dev_sum(natural):
            chunks = natural.reshape(4, rows // 4, n_dev, share).transpose(2, 1, 0, 3)
            return unfold(jnp.sum(swap(chunks.reshape(n_dev, rows // 4, 4 * share), DEV), 0), 4)

        has_parent = parents[0] < live
        right0, right1 = leaf_right[:, :width], leaf_right[:, width:]
        solved0 = jnp.where(live > 0, mm(right0, leaf_inverse[0]), 0.0)
        lifted = jnp.where(has_parent, mm(solved0, leaf_link[0]), 0.0)
        solved1 = jnp.where(live > 1, mm(right1 - lifted, leaf_inverse[1]), 0.0)
        given0, given1 = mm(solved0, leaf_front[0]), mm(solved1, leaf_front[1])
        slots = jnp.arange(n_front, dtype=jnp.int32)[None, :, None]
        placed = jnp.where(slots == front_rows[0], given0[:, None, :], 0.0) + jnp.where(
            slots == front_rows[1], given1[:, None, :], 0.0
        )
        behind = (n_x - my_x) % n_x
        spots = [my_x * (n_core * share), my_x * some]
        spots += [behind * size for size in (n_core * share, share, some)]
        for step in range(n_x):
            spot = my_z * part + (my_x + n_x - step) % n_x * (n_core * share) + my_core * share
            spots += [spot, spot + front_order]
        spots += [front_rows[block] * width for block in range(2)]
        spots = tuple(spot.astype(jnp.uint32) for spot in spots)
        placed, spots = lax.optimization_barrier((placed, spots))
        ahead_part, rows_x, back_part, back_share, back_rows = spots[:5]
        root_spots, leaf_spots = spots[5:-2], spots[-2:]
        start = front_right - dev_sum(placed.reshape(rows, front_order))
        y_own = dev_sum(mm(start, front_inverse))
        side = jnp.pad(y_own, ((0, 0), (0, width - share)))
        couples = from_all(jnp.concatenate([front_couple, side], 1))

        picks = my_dev * share + jnp.arange(share, dtype=jnp.int32)
        picks = jnp.concatenate([picks, front_order + picks])[:, None]
        picks = picks == jnp.arange(2 * front_order, dtype=jnp.int32)[None, :]
        picks = jnp.where(picks & (lax.axis_index("grp") == 0), 1.0, 0.0).astype(jnp.float32)
        fed = jnp.concatenate([-y_own, root_right[:, 0], root_right[:, 1]], 1)
        given = mm(fed, jnp.concatenate([front_couple, picks], 0))
        chunks = given.reshape(n_near, few, 2, n_z, part).transpose(3, 0, 2, 1, 4)
        given = jnp.sum(swap(chunks.reshape(n_dev, 2 * few, part), DEV), 0)
        given = reduce_over(given, "grp", n_grp)

        given = turn(given, 1, ahead_part)
        low, high = given[:few], given[few:]
        y_high = reduce_over(mm(high, w_high), "z", n_z)
        low = low - reduce_over(mmt(y_high, link), "grp", n_grp)
        y_low = reduce_over(mm(low, w_low), "z", n_z)
        x_low = reduce_over(mmt(y_low, w_low), "grp", n_grp)
        joined = jnp.concatenate([piece[:, : 2 * front_order] for piece in couples], 0)
        inverse = jnp.concatenate(inverses, 0)
        y_some = [
            lax.dynamic_slice_in_dim(piece[:, 2 * front_order :], rows_x, some, 0)[:, :share]
            for piece in couples
        ]
        y_some = jnp.concatenate(y_some, 1)
        x_low, joined, inverse, y_some = lax.optimization_barrier((x_low, joined, inverse, y_some))
        y_high = y_high - reduce_over(mm(x_low, link), "z", n_z)
        x_high = reduce_over(mmt(y_high, w_high), "grp", n_grp)

        both = turn(jnp.concatenate([x_low, x_high], 0), 1, back_part)
        whole = spread(both, LINE, n_line)
        whole = whole.reshape(n_z, n_core, 2, few, part).transpose(1, 3, 2, 0, 4)
        whole = whole.reshape(some, 2 * front_order)
        rest = turn(y_some - mmt(whole, joined), 1, back_share)
        rest = spread(rest, LINE, n_line)
        rest = rest.reshape(n_z, n_core, some, n_x, share).transpose(2, 0, 3, 1, 4)
        found = turn(mmt(rest.reshape(some, front_order), inverse), 1, back_share)
        found = spread(found, DEV, n_dev).reshape(n_z, n_x, n_core, some, n_x, share)
        front_solution = found.transpose(1, 3, 0, 4, 2, 5).reshape(rows, front_order)
        root = [
            jnp.concatenate(
                [
                    lax.dynamic_slice_in_dim(whole, spot, share, 1)
                    for spot in root_spots[2 * step : 2 * step + 2]
                ],
                1,
            )
            for step in range(n_x)
        ]
        root = [root[0]] + [from_right(root[step], step) for step in range(1, n_x)]
        root = turn(jnp.concatenate(root, 0), 0, back_rows).reshape(rows, 2, share)

        def back(solved, block):
            picked = lax.dynamic_slice_in_dim(front_solution, leaf_spots[block], width, 1)
            return solved - mmt(picked, leaf_front[block])

        base0, base1 = back(solved0, 0), back(solved1, 1)
        leaf1 = jnp.where(live > 1, mmt(base1, leaf_inverse[1]), 0.0)
        carried = jnp.where(has_parent, mmt(leaf1, leaf_link[0]), 0.0)
        leaf0 = jnp.where(live > 0, mmt(base0 - carried, leaf_inverse[0]), 0.0)
        leaf_solution = jnp.concatenate([leaf0, leaf1], 1)
        return leaf_solution, front_solution, root

    return body


def solution(mesh):
    n_grp, n_dev = mesh.shape["grp"], mesh.shape["dev"]
    fine = Mesh(mesh.devices.reshape(n_grp, n_dev // 8, 4, 2), ("grp", "z", "x", "core"))
    every = ("grp",) + DEV
    in_specs = (
        P(None, every),
        P(every, None, None),
        P(every, None, None),
        P(every, None, None),
        P(every),
        P(every),
        P(every),
        P(None, every),
        P(every, None),
        P(every, None),
        P(None, None, DEV),
        P(None, DEV, "grp"),
        P(None, DEV, "grp"),
    )
    out_specs = (P(None, every), P(None, "grp"), P(None, None, DEV))
    inner = make_body(dict(fine.shape))

    return jax.shard_map(inner, mesh=fine, in_specs=in_specs, out_specs=out_specs, check_vma=False)
```

```python
import jax
import jax.numpy as jnp
from jax import lax
from jax.experimental import pallas as pl
from jax.experimental.pallas import tpu as pltpu
from jax.sharding import Mesh
from jax.sharding import PartitionSpec as P


EXACT = lax.Precision.HIGHEST
DEV = ("z", "x", "core")
LINE = ("z", "core")


def mm(left, right):
    return jnp.dot(left, right, precision=EXACT)


def mmt(left, right):
    return jnp.einsum("rn,mn->rm", left, right, precision=EXACT)


def swap(chunks, axes):
    return lax.all_to_all(chunks, axes, 0, 0, tiled=True)


def spread(values, axes, count):
    return swap(jnp.broadcast_to(values[None], (count,) + values.shape), axes)


def reduce_over(values, axes, count):
    return jnp.sum(spread(values, axes, count), 0)


def unfold(values, folds):
    tall, width = values.shape
    thin = width // folds
    return values.reshape(tall, folds, thin).transpose(1, 0, 2).reshape(folds * tall, thin)


def leaf_forward(parents, targets, live, right, inverse, link, front, solved, chunks):
    rows, width = right.shape[0], inverse.shape[1]
    folds = chunks.shape[2] // (width // 4)
    tall = rows // folds
    alive = jnp.full((rows, width), live[0], jnp.int32)
    first = jnp.where(alive > 0, mm(right[:, :width], inverse[0]), 0.0)
    lifted = jnp.where(alive > parents[0], mm(first, link[0]), 0.0)
    second = jnp.where(alive > 1, mm(right[:, width:] - lifted, inverse[1]), 0.0)
    solved[:, :width] = first
    solved[:, width:] = second
    chunks[...] = jnp.zeros(chunks.shape, jnp.float32)
    lane = lax.broadcasted_iota(jnp.int32, (tall, width), 1)
    for block, values in enumerate((first, second)):
        given = mm(values, front[block])
        for piece in range(4):
            made = jnp.zeros((tall, width), jnp.float32)
            for fold in range(folds):
                move = (fold - piece) * (width // 4) % width
                moved = given[fold * tall : (fold + 1) * tall]
                moved = pltpu.roll(moved, move, 1) if move else moved
                inside = (lane >= fold * (width // 4)) & (lane < (fold + 1) * (width // 4))
                made = jnp.where(inside, moved, made)
            spot = targets[block] * 4 + piece
            chunks[spot] = chunks[spot] + made


def whole_block(array, space=None):
    zeros = (0,) * array.ndim
    if space is not None:
        return pl.BlockSpec(memory_space=space)
    return pl.BlockSpec(array.shape, lambda i: zeros)


def leaf_start(parents, targets, live, right, inverse, link, front, n_dev):
    rows, span = right.shape
    outs = (
        jax.ShapeDtypeStruct((rows, span), jnp.float32),
        jax.ShapeDtypeStruct((n_dev, rows // 4, 128), jnp.float32),
    )
    scalars, arrays = (parents, targets, live), (right, inverse, link, front)
    specs = [whole_block(item, pltpu.SMEM) for item in scalars]
    specs += [whole_block(item) for item in arrays]
    return pl.pallas_call(
        leaf_forward,
        grid=(1,),
        in_specs=specs,
        out_specs=tuple(whole_block(item) for item in outs),
        out_shape=outs,
    )(*scalars, *arrays)


def make_body(sizes):
    n_grp, n_z = sizes["grp"], sizes["z"]
    n_x, n_core = sizes["x"], sizes["core"]
    n_near, n_line = n_x * n_core, n_z * n_core
    n_dev = n_z * n_near

    def body(
        leaf_right,
        leaf_inverse,
        leaf_link,
        leaf_front,
        parents,
        front_rows,
        live_blocks,
        front_right,
        front_inverse,
        front_couple,
        root_right,
        root_inverse,
        root_couple,
    ):
        rows = leaf_right.shape[0]
        width = leaf_inverse.shape[1]
        front_order = front_inverse.shape[1]
        share = front_inverse.shape[0]
        part = root_inverse.shape[2]
        few = rows // n_near
        live = live_blocks[0]
        my_dev = lax.axis_index(DEV)
        my_z, my_x, my_core = (lax.axis_index(name) for name in DEV)
        some = rows // n_x

        def from_right(values, step):
            pairs = [((i + step) % n_x, i) for i in range(n_x)]
            return lax.ppermute(values, "x", pairs)

        def turn(values, axis, start):
            doubled = jnp.concatenate([values, values], axis)
            return lax.dynamic_slice_in_dim(doubled, start, values.shape[axis], axis)

        def from_all(values):
            return [values] + [from_right(values, step) for step in range(1, n_x)]

        chain = from_all(jnp.concatenate([root_inverse, root_couple], 0))
        chain = lax.all_gather(jnp.stack(chain, 0), "core", axis=0)
        chain = [
            chain[:, :, item].transpose(1, 0, 2, 3).reshape(n_near * share, part)
            for item in range(3)
        ]
        w_low, w_high, link = lax.optimization_barrier(tuple(chain))
        inverses = from_all(front_inverse)

        def dev_sum(natural):
            chunks = natural.reshape(4, rows // 4, n_dev, share).transpose(2, 1, 0, 3)
            return unfold(jnp.sum(swap(chunks.reshape(n_dev, rows // 4, 4 * share), DEV), 0), 4)

        has_parent = parents[0] < live
        solved, placed = leaf_start(
            parents, front_rows, live_blocks, leaf_right, leaf_inverse, leaf_link, leaf_front, n_dev
        )
        solved0, solved1 = solved[:, :width], solved[:, width:]
        behind = (n_x - my_x) % n_x
        spots = [my_x * (n_core * share), my_x * some]
        spots += [behind * size for size in (n_core * share, share, some)]
        for step in range(n_x):
            spot = my_z * part + (my_x + n_x - step) % n_x * (n_core * share) + my_core * share
            spots += [spot, spot + front_order]
        spots += [front_rows[block] * width for block in range(2)]
        spots = tuple(spot.astype(jnp.uint32) for spot in spots)
        start = front_right - unfold(jnp.sum(swap(placed, DEV), 0), 4)
        start, spots = lax.optimization_barrier((start, spots))
        ahead_part, rows_x, back_part, back_share, back_rows = spots[:5]
        root_spots, leaf_spots = spots[5:-2], spots[-2:]
        y_own = dev_sum(mm(start, front_inverse))
        side = jnp.pad(y_own, ((0, 0), (0, width - share)))
        couples = from_all(jnp.concatenate([front_couple, side], 1))

        picks = my_dev * share + jnp.arange(share, dtype=jnp.int32)
        picks = jnp.concatenate([picks, front_order + picks])[:, None]
        picks = picks == jnp.arange(2 * front_order, dtype=jnp.int32)[None, :]
        picks = jnp.where(picks & (lax.axis_index("grp") == 0), 1.0, 0.0).astype(jnp.float32)
        fed = jnp.concatenate([-y_own, root_right[:, 0], root_right[:, 1]], 1)
        given = mm(fed, jnp.concatenate([front_couple, picks], 0))
        chunks = given.reshape(n_near, few, 2, n_z, part).transpose(3, 0, 2, 1, 4)
        given = jnp.sum(swap(chunks.reshape(n_dev, 2 * few, part), DEV), 0)
        given = reduce_over(given, "grp", n_grp)

        given = turn(given, 1, ahead_part)
        low, high = given[:few], given[few:]
        y_high = reduce_over(mm(high, w_high), "z", n_z)
        low = low - reduce_over(mmt(y_high, link), "grp", n_grp)
        y_low = reduce_over(mm(low, w_low), "z", n_z)
        x_low = reduce_over(mmt(y_low, w_low), "grp", n_grp)
        joined = jnp.concatenate([piece[:, : 2 * front_order] for piece in couples], 0)
        inverse = jnp.concatenate(inverses, 0)
        y_some = [
            lax.dynamic_slice_in_dim(piece[:, 2 * front_order :], rows_x, some, 0)[:, :share]
            for piece in couples
        ]
        y_some = jnp.concatenate(y_some, 1)
        x_low, joined, inverse, y_some = lax.optimization_barrier((x_low, joined, inverse, y_some))
        y_high = y_high - reduce_over(mm(x_low, link), "z", n_z)
        x_high = reduce_over(mmt(y_high, w_high), "grp", n_grp)

        both = turn(jnp.concatenate([x_low, x_high], 0), 1, back_part)
        whole = spread(both, LINE, n_line)
        whole = whole.reshape(n_z, n_core, 2, few, part).transpose(1, 3, 2, 0, 4)
        whole = whole.reshape(some, 2 * front_order)
        rest = turn(y_some - mmt(whole, joined), 1, back_share)
        rest = spread(rest, LINE, n_line)
        rest = rest.reshape(n_z, n_core, some, n_x, share).transpose(2, 0, 3, 1, 4)
        found = turn(mmt(rest.reshape(some, front_order), inverse), 1, back_share)
        found = spread(found, DEV, n_dev).reshape(n_z, n_x, n_core, some, n_x, share)
        front_solution = found.transpose(1, 3, 0, 4, 2, 5).reshape(rows, front_order)
        root = [
            jnp.concatenate(
                [
                    lax.dynamic_slice_in_dim(whole, spot, share, 1)
                    for spot in root_spots[2 * step : 2 * step + 2]
                ],
                1,
            )
            for step in range(n_x)
        ]
        root = [root[0]] + [from_right(root[step], step) for step in range(1, n_x)]
        root = turn(jnp.concatenate(root, 0), 0, back_rows).reshape(rows, 2, share)

        def back(solved, block):
            picked = lax.dynamic_slice_in_dim(front_solution, leaf_spots[block], width, 1)
            return solved - mmt(picked, leaf_front[block])

        base0, base1 = back(solved0, 0), back(solved1, 1)
        leaf1 = jnp.where(live > 1, mmt(base1, leaf_inverse[1]), 0.0)
        carried = jnp.where(has_parent, mmt(leaf1, leaf_link[0]), 0.0)
        leaf0 = jnp.where(live > 0, mmt(base0 - carried, leaf_inverse[0]), 0.0)
        leaf_solution = jnp.concatenate([leaf0, leaf1], 1)
        return leaf_solution, front_solution, root

    return body


def solution(mesh):
    n_grp, n_dev = mesh.shape["grp"], mesh.shape["dev"]
    fine = Mesh(mesh.devices.reshape(n_grp, n_dev // 8, 4, 2), ("grp", "z", "x", "core"))
    every = ("grp",) + DEV
    in_specs = (
        P(None, every),
        P(every, None, None),
        P(every, None, None),
        P(every, None, None),
        P(every),
        P(every),
        P(every),
        P(None, every),
        P(every, None),
        P(every, None),
        P(None, None, DEV),
        P(None, DEV, "grp"),
        P(None, DEV, "grp"),
    )
    out_specs = (P(None, every), P(None, "grp"), P(None, None, DEV))
    inner = make_body(dict(fine.shape))

    return jax.shard_map(inner, mesh=fine, in_specs=in_specs, out_specs=out_specs, check_vma=False)
```

```python
import jax
import jax.numpy as jnp
from jax import lax
from jax.experimental import pallas as pl
from jax.experimental.pallas import tpu as pltpu
from jax.sharding import Mesh
from jax.sharding import PartitionSpec as P


EXACT = lax.Precision.HIGHEST
DEV = ("z", "x", "core")
LINE = ("z", "core")


def mm(left, right):
    return jnp.dot(left, right, precision=EXACT)


def mmt(left, right):
    return jnp.einsum("rn,mn->rm", left, right, precision=EXACT)


def swap(chunks, axes):
    return lax.all_to_all(chunks, axes, 0, 0, tiled=True)


def spread(values, axes, count):
    return swap(jnp.broadcast_to(values[None], (count,) + values.shape), axes)


def reduce_over(values, axes, count):
    return jnp.sum(spread(values, axes, count), 0)


def unfold(values, folds):
    tall, width = values.shape
    thin = width // folds
    return values.reshape(tall, folds, thin).transpose(1, 0, 2).reshape(folds * tall, thin)


def leaf_forward(parents, targets, live, right, inverse, link, front, solved, chunks):
    rows, width = right.shape[0], inverse.shape[1]
    folds = chunks.shape[2] // (width // 4)
    tall = rows // folds
    alive = jnp.full((rows, width), live[0], jnp.int32)
    first = jnp.where(alive > 0, mm(right[:, :width], inverse[0]), 0.0)
    lifted = jnp.where(alive > parents[0], mm(first, link[0]), 0.0)
    second = jnp.where(alive > 1, mm(right[:, width:] - lifted, inverse[1]), 0.0)
    solved[:, :width] = first
    solved[:, width:] = second
    chunks[...] = jnp.zeros(chunks.shape, jnp.float32)
    lane = lax.broadcasted_iota(jnp.int32, (tall, width), 1)
    for block, values in enumerate((first, second)):
        given = mm(values, front[block])
        for piece in range(4):
            made = jnp.zeros((tall, width), jnp.float32)
            for fold in range(folds):
                move = (fold - piece) * (width // 4) % width
                moved = given[fold * tall : (fold + 1) * tall]
                moved = pltpu.roll(moved, move, 1) if move else moved
                inside = (lane >= fold * (width // 4)) & (lane < (fold + 1) * (width // 4))
                made = jnp.where(inside, moved, made)
            spot = targets[block] * 4 + piece
            chunks[spot] = chunks[spot] + made


def leaf_backward(parents, targets, live, parts, solved, inverse, link, front, leaf, fronts):
    rows, width = solved.shape[0], inverse.shape[1]
    n_z, n_x, _, tall, span = parts.shape
    share = span // n_x
    lane = lax.broadcasted_iota(jnp.int32, (n_z * n_x * tall, span), 1)
    for half in range(2):
        made = jnp.zeros((n_z * n_x * tall, span), jnp.float32)
        for piece in range(4):
            source = half * 2 + piece // 2
            moved = parts[:, :, piece % 2].reshape(n_z * n_x * tall, span)
            move = (piece - source) * share % span
            moved = pltpu.roll(moved, move, 1) if move else moved
            inside = (lane >= piece * share) & (lane < (piece + 1) * share)
            made = jnp.where(inside, moved, made)
        made = made.reshape(n_z, n_x * tall, span)
        for z in range(n_z):
            fronts[:, (2 * z + half) * width : (2 * z + half + 1) * width] = made[z]
    alive = jnp.full((rows, width), live[0], jnp.int32)
    base = []
    for block in range(2):
        spot = pl.multiple_of(targets[block] * width, width)
        picked = fronts[:, pl.ds(spot, width)]
        base.append(solved[:, block * width : (block + 1) * width] - mmt(picked, front[block]))
    second = jnp.where(alive > 1, mmt(base[1], inverse[1]), 0.0)
    carried = jnp.where(alive > parents[0], mmt(second, link[0]), 0.0)
    leaf[:, :width] = jnp.where(alive > 0, mmt(base[0] - carried, inverse[0]), 0.0)
    leaf[:, width:] = second


def leaf_end(parents, targets, live, parts, solved, inverse, link, front, front_order):
    rows, span = solved.shape
    outs = (
        jax.ShapeDtypeStruct((rows, span), jnp.float32),
        jax.ShapeDtypeStruct((rows, front_order), jnp.float32),
    )
    scalars, arrays = (parents, targets, live), (parts, solved, inverse, link, front)
    specs = [whole_block(item, pltpu.SMEM) for item in scalars]
    specs += [whole_block(item) for item in arrays]
    return pl.pallas_call(
        leaf_backward,
        grid=(1,),
        in_specs=specs,
        out_specs=tuple(whole_block(item) for item in outs),
        out_shape=outs,
    )(*scalars, *arrays)


def whole_block(array, space=None):
    zeros = (0,) * array.ndim
    if space is not None:
        return pl.BlockSpec(memory_space=space)
    return pl.BlockSpec(array.shape, lambda i: zeros)


def leaf_start(parents, targets, live, right, inverse, link, front, n_dev):
    rows, span = right.shape
    outs = (
        jax.ShapeDtypeStruct((rows, span), jnp.float32),
        jax.ShapeDtypeStruct((n_dev, rows // 4, 128), jnp.float32),
    )
    scalars, arrays = (parents, targets, live), (right, inverse, link, front)
    specs = [whole_block(item, pltpu.SMEM) for item in scalars]
    specs += [whole_block(item) for item in arrays]
    return pl.pallas_call(
        leaf_forward,
        grid=(1,),
        in_specs=specs,
        out_specs=tuple(whole_block(item) for item in outs),
        out_shape=outs,
    )(*scalars, *arrays)


def make_body(sizes):
    n_grp, n_z = sizes["grp"], sizes["z"]
    n_x, n_core = sizes["x"], sizes["core"]
    n_near, n_line = n_x * n_core, n_z * n_core
    n_dev = n_z * n_near

    def body(
        leaf_right,
        leaf_inverse,
        leaf_link,
        leaf_front,
        parents,
        front_rows,
        live_blocks,
        front_right,
        front_inverse,
        front_couple,
        root_right,
        root_inverse,
        root_couple,
    ):
        rows = leaf_right.shape[0]
        width = leaf_inverse.shape[1]
        front_order = front_inverse.shape[1]
        share = front_inverse.shape[0]
        part = root_inverse.shape[2]
        few = rows // n_near
        my_dev = lax.axis_index(DEV)
        my_z, my_x, my_core = (lax.axis_index(name) for name in DEV)
        some = rows // n_x

        def from_right(values, step):
            pairs = [((i + step) % n_x, i) for i in range(n_x)]
            return lax.ppermute(values, "x", pairs)

        def turn(values, axis, start):
            doubled = jnp.concatenate([values, values], axis)
            return lax.dynamic_slice_in_dim(doubled, start, values.shape[axis], axis)

        def from_all(values):
            return [values] + [from_right(values, step) for step in range(1, n_x)]

        chain = from_all(jnp.concatenate([root_inverse, root_couple], 0))
        chain = lax.all_gather(jnp.stack(chain, 0), "core", axis=0)
        chain = [
            chain[:, :, item].transpose(1, 0, 2, 3).reshape(n_near * share, part)
            for item in range(3)
        ]
        w_low, w_high, link = lax.optimization_barrier(tuple(chain))
        inverses = from_all(front_inverse)

        def dev_sum(natural):
            chunks = natural.reshape(4, rows // 4, n_dev, share).transpose(2, 1, 0, 3)
            return unfold(jnp.sum(swap(chunks.reshape(n_dev, rows // 4, 4 * share), DEV), 0), 4)

        solved, placed = leaf_start(
            parents, front_rows, live_blocks, leaf_right, leaf_inverse, leaf_link, leaf_front, n_dev
        )
        behind = (n_x - my_x) % n_x
        spots = [my_x * (n_core * share), my_x * some]
        spots += [behind * size for size in (n_core * share, share, some)]
        for step in range(n_x):
            spot = my_z * part + (my_x + n_x - step) % n_x * (n_core * share) + my_core * share
            spots += [spot, spot + front_order]
        spots = tuple(spot.astype(jnp.uint32) for spot in spots)
        start = front_right - unfold(jnp.sum(swap(placed, DEV), 0), 4)
        start, spots = lax.optimization_barrier((start, spots))
        ahead_part, rows_x, back_part, back_share, back_rows = spots[:5]
        root_spots = spots[5:]
        y_own = dev_sum(mm(start, front_inverse))
        side = jnp.pad(y_own, ((0, 0), (0, width - share)))
        couples = from_all(jnp.concatenate([front_couple, side], 1))

        picks = my_dev * share + jnp.arange(share, dtype=jnp.int32)
        picks = jnp.concatenate([picks, front_order + picks])[:, None]
        picks = picks == jnp.arange(2 * front_order, dtype=jnp.int32)[None, :]
        picks = jnp.where(picks & (lax.axis_index("grp") == 0), 1.0, 0.0).astype(jnp.float32)
        fed = jnp.concatenate([-y_own, root_right[:, 0], root_right[:, 1]], 1)
        given = mm(fed, jnp.concatenate([front_couple, picks], 0))
        chunks = given.reshape(n_near, few, 2, n_z, part).transpose(3, 0, 2, 1, 4)
        given = jnp.sum(swap(chunks.reshape(n_dev, 2 * few, part), DEV), 0)
        given = reduce_over(given, "grp", n_grp)

        given = turn(given, 1, ahead_part)
        low, high = given[:few], given[few:]
        y_high = reduce_over(mm(high, w_high), "z", n_z)
        low = low - reduce_over(mmt(y_high, link), "grp", n_grp)
        y_low = reduce_over(mm(low, w_low), "z", n_z)
        x_low = reduce_over(mmt(y_low, w_low), "grp", n_grp)
        joined = jnp.concatenate([piece[:, : 2 * front_order] for piece in couples], 0)
        inverse = jnp.concatenate(inverses, 0)
        y_some = [
            lax.dynamic_slice_in_dim(piece[:, 2 * front_order :], rows_x, some, 0)[:, :share]
            for piece in couples
        ]
        y_some = jnp.concatenate(y_some, 1)
        x_low, joined, inverse, y_some = lax.optimization_barrier((x_low, joined, inverse, y_some))
        y_high = y_high - reduce_over(mm(x_low, link), "z", n_z)
        x_high = reduce_over(mmt(y_high, w_high), "grp", n_grp)

        both = turn(jnp.concatenate([x_low, x_high], 0), 1, back_part)
        whole = spread(both, LINE, n_line)
        whole = whole.reshape(n_z, n_core, 2, few, part).transpose(1, 3, 2, 0, 4)
        whole = whole.reshape(some, 2 * front_order)
        rest = turn(y_some - mmt(whole, joined), 1, back_share)
        rest = spread(rest, LINE, n_line)
        rest = rest.reshape(n_z, n_core, some, n_x, share).transpose(2, 0, 3, 1, 4)
        found = turn(mmt(rest.reshape(some, front_order), inverse), 1, back_share)
        found = spread(found, DEV, n_dev).reshape(n_z, n_x, n_core, some, n_x * share)
        root = []
        early = lax.optimization_barrier(whole)
        for step in range(n_x):
            cuts = root_spots[2 * step : 2 * step + 2]
            cuts = [lax.dynamic_slice_in_dim(early if step in (1, 3) else whole, spot, share, 1) for spot in cuts]
            cuts = jnp.concatenate(cuts, 1)
            root.append(from_right(cuts, step) if step else cuts)
        root = turn(jnp.concatenate(root, 0), 0, back_rows).reshape(rows, 2, share)

        leaf_solution, front_solution = leaf_end(
            parents, front_rows, live_blocks, found, solved, leaf_inverse, leaf_link, leaf_front,
            front_order,
        )
        return leaf_solution, front_solution, root

    return body


def solution(mesh):
    n_grp, n_dev = mesh.shape["grp"], mesh.shape["dev"]
    fine = Mesh(mesh.devices.reshape(n_grp, n_dev // 8, 4, 2), ("grp", "z", "x", "core"))
    every = ("grp",) + DEV
    in_specs = (
        P(None, every),
        P(every, None, None),
        P(every, None, None),
        P(every, None, None),
        P(every),
        P(every),
        P(every),
        P(None, every),
        P(every, None),
        P(every, None),
        P(None, None, DEV),
        P(None, DEV, "grp"),
        P(None, DEV, "grp"),
    )
    out_specs = (P(None, every), P(None, "grp"), P(None, None, DEV))
    inner = make_body(dict(fine.shape))

    return jax.shard_map(inner, mesh=fine, in_specs=in_specs, out_specs=out_specs, check_vma=False)
```
